32 devices in a mesh: groups: 2 (over x), tile: 16 (over z, y, core).
Axes of the slice: x: 2, y: 2, z: 4, core: 2. Of those that a mesh axis runs over, the one named last changes fastest.
Arguments:
- data_halves: bfloat16 [2, 4, 256, 32, 512], P(None, None, ('groups', 'tile')), parts along dimension 2, may hold values from 0.1 to 20, as said below
- psf_taps: float32 [4, 3, 9], replicated, may hold values from 0.05 to 1
- cycle_map: int32 [32, 32, 512], P(('groups', 'tile')), parts along dimension 0, may hold values from 0 to 255, as said below
- cutoff: int32 [2], P('groups'), parts along dimension 0, may hold values from 64 to 255
Outputs:
- joined: float32 [256, 32, 512], P(('groups', 'tile')), parts along dimension 0
The draws below stay inside these ranges and needn't reach their ends.
There are 2 independent parts, one for each index of `groups`. The reference program is written for one: setup_inputs(seed, part) draws one part's arguments, and reference() takes and returns one part's arrays. A program takes and returns all parts, laid end to end along the dimension named above; an argument that names none is the same for every part. Nothing has to cross between parts.
Inputs may be any that keep to these rules, and one draw needn't show every extreme that they name: `data_halves`: positive photon counts. cycle_map[b, k, l] is the cycle of frequency (k, l) in block b: with fk = min(k, 32 - k), fl = min(l, 512 - l) and a whole stretch s_b of 1 to 4 drawn for each block, the largest r with r * r <= (s_b fk)^2 + fl^2, capped at 255.
All inputs are finite; a program needn't handle non-finite values.
Results may differ from the reference program's by a relative error of at most 0.00095.
The reference program's roundings to bfloat16 on the way count: a program that leaves them out, or rounds other values in their place, can miss the bound.
Values may be sent and summed in bfloat16 or wider, within the bound.
No kernel may reach another device: no remote copies, remote signals or barrier semaphores. Data moves between devices by JAX's collectives and lax.ppermute only.
A program may use at most 64 MiB of HBM per device.

```python
import math
import jax
import jax.numpy as jnp
from jax import lax

SLAB = 8
DEPTH = 32
LATERAL = 512
VIEWS = 4
TAPS = 9
ITERS = 2
CYCLES = 256
BLOCKS = 16
EXTENT = 128


def draw_data_halves(key, part):
    key_signal, key_noise, key_place = jax.random.split(jax.random.fold_in(key, 11), 3)
    position = jnp.arange(EXTENT).astype(jnp.float32) / EXTENT
    profile = jnp.exp(jnp.log(4.0) * position)[:, None, None]
    signal = jnp.clip(jnp.exp(0.4 * jax.random.normal(key_signal, (EXTENT, DEPTH, LATERAL), jnp.float32)), 0.2, 3.0)
    quarter = jax.random.randint(key_place, (), 1, 4)
    row_quarter = jnp.arange(EXTENT) * 4 // EXTENT
    strength = jnp.where(row_quarter == quarter, 0.5, 0.05).astype(jnp.float32)
    unit_noise = jax.random.uniform(key_noise, (2, VIEWS, EXTENT, DEPTH, LATERAL), jnp.float32, -1.0, 1.0)
    shot_noise = 1.0 + strength[None, None, :, None, None] * unit_noise
    return (profile * signal * shot_noise).astype(jnp.bfloat16)


def draw_cycle_map(key, part):
    stretch = jax.random.randint(jax.random.fold_in(key, 23), (BLOCKS,), 1, 5)
    index_z = jnp.arange(DEPTH)
    index_y = jnp.arange(LATERAL)
    fold_z = jnp.minimum(index_z, DEPTH - index_z)
    fold_y = jnp.minimum(index_y, LATERAL - index_y)
    scaled = stretch[:, None] * fold_z[None, :]
    radius_sq = scaled[:, :, None] ** 2 + (fold_y ** 2)[None, None, :]
    lowest = jnp.zeros_like(radius_sq)
    for bit_number in range(12, -1, -1):
        candidate = lowest + (1 << bit_number)
        lowest = jnp.where(candidate * candidate <= radius_sq, candidate, lowest)
    cycle = jnp.minimum(lowest, CYCLES - 1)
    return cycle.astype(jnp.int32)


def setup_inputs(seed: int = 0, part: int = 0) -> dict:
    seeds = jax.random.split(jax.random.key(seed), 5)
    own_keys = jax.random.split(jax.random.fold_in(seeds[4], part), 5)
    return {
        "data_halves": draw_data_halves(jax.random.fold_in(jax.random.fold_in(seeds[4], part), 71), part),
        "psf_taps": jnp.clip(jnp.exp(jax.random.uniform(seeds[1], (VIEWS, 3, TAPS), jnp.float32, math.log(0.05), math.log(1.0))), 0.05, 1.0),
        "cycle_map": draw_cycle_map(jax.random.fold_in(jax.random.fold_in(seeds[4], part), 71), part),
        "cutoff": jax.random.randint(own_keys[3], (1,), CYCLES // 4, CYCLES).astype(jnp.int32),
    }


highest = lax.Precision.HIGHEST

def conv_axis(volume, kernel, along):
    radius = kernel.shape[-1] // 2
    length = volume.shape[along]
    widths = [(0, 0)] * volume.ndim
    widths[along] = (radius, radius)
    padded = jnp.pad(volume, widths)
    summed = jnp.zeros_like(volume)
    for tap_index in range(kernel.shape[-1]):
        shifted = lax.slice_in_dim(padded, tap_index, tap_index + length, axis=along)
        summed = summed + kernel[:, tap_index][:, None, None, None] * shifted
    return summed

def blur_field(volume, kernels):
    volume = conv_axis(volume, kernels[:, 0], 1)
    volume = conv_axis(volume, kernels[:, 1], 2)
    return conv_axis(volume, kernels[:, 2], 3)

def tables(length):
    index_n = jnp.arange(length)
    phase = index_n[:, None] * index_n[None, :] % length
    angle = phase.astype(jnp.float32) * (2.0 * jnp.pi / length)
    return (jnp.cos(angle), jnp.sin(angle))

def reference(data_halves, psf_taps, cycle_map, cutoff):
    kernels = psf_taps / lax.optimization_barrier(jnp.sum(psf_taps, axis=-1, keepdims=True))
    mirrored = kernels[:, :, ::-1]
    cos_z, sin_z = tables(DEPTH)
    cos_full, sin_full = tables(LATERAL)
    lat_cos = cos_full.astype(jnp.bfloat16)
    lat_sin = sin_full.astype(jnp.bfloat16)
    reals = []
    imags = []
    for half_index in range(2):
        observed = data_halves[half_index].astype(jnp.float32)
        estimate = lax.optimization_barrier(jnp.mean(observed, axis=0))
        for iteration in range(ITERS):
            predicted = blur_field(jnp.broadcast_to(estimate[None], observed.shape), kernels)
            correction = blur_field(observed / predicted, mirrored)
            estimate = estimate * lax.optimization_barrier(jnp.mean(correction, axis=0))
        rounded = estimate.astype(jnp.bfloat16).reshape(-1, LATERAL)
        row_real = jnp.dot(rounded, lat_cos, preferred_element_type=jnp.float32).reshape(EXTENT, DEPTH, LATERAL)
        row_imag = -jnp.dot(rounded, lat_sin, preferred_element_type=jnp.float32).reshape(EXTENT, DEPTH, LATERAL)
        spec_real = jnp.einsum('kz,xzl->xkl', cos_z, row_real, precision=highest) + jnp.einsum('kz,xzl->xkl', sin_z, row_imag, precision=highest)
        spec_imag = jnp.einsum('kz,xzl->xkl', cos_z, row_imag, precision=highest) - jnp.einsum('kz,xzl->xkl', sin_z, row_real, precision=highest)
        reals.append(spec_real)
        imags.append(spec_imag)
    cross_power = reals[0] * reals[1] + imags[0] * imags[1]
    power_a = reals[0] ** 2 + imags[0] ** 2
    power_b = reals[1] ** 2 + imags[1] ** 2
    cycle_ids = cycle_map.reshape(-1)

    def cycle_total(values):
        per_block = lax.optimization_barrier(jnp.sum(values.reshape(BLOCKS, SLAB, DEPTH, LATERAL), axis=1))
        return jax.ops.segment_sum(per_block.reshape(-1), cycle_ids, CYCLES)
    numerator = cycle_total(cross_power)
    cycle_corr = numerator / (jnp.sqrt(cycle_total(power_a)) * jnp.sqrt(cycle_total(power_b)))
    cycle_weight = jnp.where(jnp.arange(CYCLES) <= cutoff[0], cycle_corr, 0.0)
    cell_weight = cycle_weight[cycle_map][:, None]
    mixed_real = ((0.5 * (reals[0] + reals[1])).reshape(BLOCKS, SLAB, DEPTH, LATERAL) * cell_weight).reshape(EXTENT, DEPTH, LATERAL)
    mixed_imag = ((0.5 * (imags[0] + imags[1])).reshape(BLOCKS, SLAB, DEPTH, LATERAL) * cell_weight).reshape(EXTENT, DEPTH, LATERAL)
    inner_real = jnp.einsum('zk,xkl->xzl', cos_z, mixed_real, precision=highest) - jnp.einsum('zk,xkl->xzl', sin_z, mixed_imag, precision=highest)
    inner_imag = jnp.einsum('zk,xkl->xzl', sin_z, mixed_real, precision=highest) + jnp.einsum('zk,xkl->xzl', cos_z, mixed_imag, precision=highest)
    inner_real = inner_real.astype(jnp.bfloat16).reshape(-1, LATERAL)
    inner_imag = inner_imag.astype(jnp.bfloat16).reshape(-1, LATERAL)
    joined = jnp.dot(inner_real, lat_cos, preferred_element_type=jnp.float32) - jnp.dot(inner_imag, lat_sin, preferred_element_type=jnp.float32)
    joined = joined.reshape(EXTENT, DEPTH, LATERAL) / (DEPTH * LATERAL)
    return joined.astype(jnp.float32)
```

```python
import jax
import jax.numpy as jnp
import numpy as np
from jax import lax
from jax.experimental import pallas as pl
from jax.experimental.pallas import tpu as pltpu
from jax.sharding import PartitionSpec as P

CYCLES = 256
BF = jnp.bfloat16
F32 = jnp.float32
VMEM_LIMIT = 32 * 1024 * 1024


def dot(a, b):
    return lax.dot_general(a, b, (((1,), (0,)), ((), ())), preferred_element_type=F32)


def iota(shape, dim):
    return lax.broadcasted_iota(jnp.int32, shape, dim)


def lookup(index, values):
    total = jnp.zeros(index.shape, F32)
    for place, value in values:
        total = jnp.where(index == place, value, total)
    return total


def shift_rows(x, by):
    count = x.shape[0]
    if by == 0:
        return x
    pad = jnp.zeros((abs(by), x.shape[1]), x.dtype)
    if by > 0:
        return jnp.concatenate([x[by:], pad], axis=0)
    return jnp.concatenate([pad, x[: count + by]], axis=0)


def prep_kernel(views, taps, slab, depth, lateral):
    radius = taps // 2
    group = 128 // depth
    ext = slab + 2 * radius
    rows = slab * depth
    scale = 1.0 / views

    def kernel(kern, place, a_ref, b_ref, t_ref, c_ref, tt_ref, ct_ref, base_ref, off_ref, row_ref, w_ref, one0_ref, one1_ref):
        first, rows_total = place[0], place[1]

        def tap(v, axis, t):
            return kern[(v * 3 + axis) * taps + t]

        def ones(v, axis, index, count, flip):
            summed = jnp.zeros(index.shape, F32)
            for t in range(taps):
                source = index + t - radius
                ok = (source >= 0) & (source < count)
                summed = summed + jnp.where(ok, tap(v, axis, taps - 1 - t if flip else t), 0.0)
            return summed

        row = iota((depth, 128), 0)
        lane = iota((depth, 128), 1)
        cell = lax.rem(lane, depth)
        slot = lane // depth
        gap_z = cell - row + radius
        gap_zt = row - cell + radius
        gap = iota((128, 128), 0) - iota((128, 128), 1) + radius
        upper_gap = gap[120:128] - 128
        lower_gap = gap[0:8] + 128
        zero = jnp.zeros((depth, 128), BF)
        flat = jnp.zeros((128, 128), BF)
        tail = jnp.zeros((120, 128), F32)
        gains = []
        for v in range(views):
            band_z = lookup(gap_z, [(t, tap(v, 1, t)) for t in range(taps)])
            band_zt = lookup(gap_zt, [(t, tap(v, 1, t)) for t in range(taps)])

            def lane_taps(shift, sign, v=v):
                pairs = [(j, shift + sign * j) for j in range(group)]
                pairs = [(j, tap(v, 0, t)) for j, t in pairs if 0 <= t < taps]
                return lookup(slot, pairs) if pairs else None

            blocks = {}
            for i in range(slab):
                for g in range(ext * depth // 128):
                    d = group * g - i
                    if d not in blocks:
                        weight = lane_taps(d, 1)
                        blocks[d] = zero if weight is None else (weight * band_z).astype(BF)
                    a_ref[pl.ds((v * slab + i) * depth, depth), pl.ds(g * 128, 128)] = blocks[d]
            blocks = {}
            for i in range(ext):
                for g in range(rows // 128):
                    d = i - group * g
                    if d not in blocks:
                        weight = lane_taps(d, -1)
                        blocks[d] = zero if weight is None else (weight * band_zt).astype(BF)
                    b_ref[pl.ds(i * depth, depth), pl.ds(v * rows + g * 128, 128)] = blocks[d]

            for flip, band_ref, cross_ref in ((False, t_ref, c_ref), (True, tt_ref, ct_ref)):
                pairs = [(t, tap(v, 2, taps - 1 - t if flip else t)) for t in range(taps)]
                middle = lookup(gap, pairs).astype(BF)
                upper = jnp.concatenate([tail, lookup(upper_gap, pairs[:radius])], axis=0).astype(BF)
                lower = jnp.concatenate([lookup(lower_gap, pairs[radius + 1 :]), tail], axis=0).astype(BF)
                for at, block in ((0, middle), (1, upper), (2, lower), (3, middle)):
                    at_rows, at_cols = pl.ds(at // 2 * 128, 128), pl.ds(at % 2 * 128, 128)
                    band_ref[v, at_rows, at_cols] = block
                    cross_ref[v, at_rows, at_cols] = flat if at in (0, 3) else block

            mid = depth // 2
            sum_xz = jnp.sum(
                a_ref[pl.ds(v * rows, depth), :].astype(F32)[mid : mid + 1], axis=1, keepdims=True
            )
            sum_y = jnp.sum(t_ref[v, 0:128, :].astype(F32)[64:65], axis=1, keepdims=True)
            gains.append(1.0 / (sum_xz * sum_y))

        def blur_z(v, x, flip):
            total = None
            for t in range(taps):
                term = shift_rows(x, t - radius) * tap(v, 1, taps - 1 - t if flip else t)
                total = term if total is None else total + term
            return total

        field0 = [ones(v, 1, row, depth, False) for v in range(views)]
        back0 = [blur_z(v, 1.0 / field0[v], True) for v in range(views)]
        shape = back0[0]
        for v in range(1, views):
            shape = shape + back0[v]
        shape = shape * scale
        w_ref[...] = shape
        field1 = [blur_z(v, shape, False) for v in range(views)]
        back1 = [blur_z(v, 1.0 / field1[v], True) for v in range(views)]

        x_out = iota((slab, 128), 0) + first
        x_ext = iota((ext, 128), 0) + (first - radius)
        y_row = iota((8, lateral), 1)
        edges = []
        for v in range(views):
            part_x = ones(v, 0, x_out, rows_total, False)
            for n, field in enumerate((field0, field1)):
                for i in range(slab):
                    at = pl.ds((v * slab + i) * depth, depth)
                    base_ref[n, at, :] = field[v] * part_x[i : i + 1]
                off_ref[n, v] = gains[v] / field[v]
            row_ref[v, 0] = ones(v, 2, y_row, lateral, False)
            row_ref[v, 1] = jnp.broadcast_to(gains[v], (8, lateral))
            edges.append((ones(v, 0, x_ext, rows_total, True) * scale, ones(v, 2, y_row, lateral, True)))
        for n, back, one_ref, low, high in (
            (0, back0, one0_ref, 0, ext),
            (1, back1, one1_ref, radius, radius + slab),
        ):
            for e in range(low, high):
                terms = [back[v] * edges[v][0][e : e + 1] for v in range(views)]
                for j in range(lateral // 128):
                    total = None
                    for v in range(views):
                        term = terms[v]
                        if j in (0, lateral // 128 - 1):
                            term = term * edges[v][1][0:1, j * 128 : (j + 1) * 128]
                        total = term if total is None else total + term
                    one_ref[pl.ds((e - low) * depth, depth), pl.ds(j * 128, 128)] = total

    return kernel


def y_blur(x, band, cross):
    left = dot(x[:, 0:256], band)
    right = dot(x[:, 256:512], band)
    mid = dot(x[:, 128:384], cross)
    left = jnp.concatenate([left[:, 0:128], left[:, 128:256] + mid[:, 0:128]], axis=1)
    right = jnp.concatenate([right[:, 0:128] + mid[:, 128:256], right[:, 128:256]], axis=1)
    return jnp.concatenate([left, right], axis=1)


def mean_views(data_ref, views):
    total = data_ref[0, 0].astype(F32)
    for v in range(1, views):
        total = total + data_ref[0, v].astype(F32)
    return total * (1.0 / views)


def level_of(x):
    total = jnp.sum(jnp.sum(x, axis=0, keepdims=True), axis=1, keepdims=True)
    return (total * (1.0 / x.size)).astype(BF).astype(F32)


def across(x, lateral):
    return jnp.concatenate([x] * (lateral // 128), axis=1)


def blur_back(n, views, slab, rows, level, data_ref, ext, mats, held):
    a_ref, b_ref, t_ref, c_ref, tt_ref, ct_ref, base_ref, off_ref, row_ref = mats
    lateral = ext.shape[1]
    for v in range(views):
        part = dot(a_ref[pl.ds(v * rows, rows), :], ext).astype(BF)
        base = across(base_ref[n, pl.ds(v * rows, rows), :], lateral) * (row_ref[v, 0, 0:1, :] * level)
        predicted = y_blur(part, t_ref[v], c_ref[v]) + base
        scaled = data_ref[0, v].astype(F32) * row_ref[v, 1, 0:1, :]
        offset = across(jnp.concatenate([off_ref[n, v]] * slab, axis=0), lateral)
        quotient = (scaled / predicted - offset).astype(BF)
        held[pl.ds(v * rows, rows), :] = y_blur(quotient, tt_ref[v], ct_ref[v]).astype(BF)
    return dot(b_ref[...], held[...])


def pick(even, from_pair, from_other):
    pair = from_pair[0].astype(F32)
    other = from_other[0].astype(F32)
    return jnp.where(even, other, pair), jnp.where(even, pair, other)


def put(even, low, high, to_pair, to_other):
    @pl.when(even)
    def _():
        to_pair[0] = high
        to_other[0] = low

    @pl.when(jnp.logical_not(even))
    def _():
        to_pair[0] = low
        to_other[0] = high


def first_kernel(views, slab, rows, edge):
    def kernel(place, data_ref, pair_ref, other_ref, *refs):
        mats, (own_ref, to_pair, to_other, held) = refs[:9], refs[9:]
        even = place[2] == 0
        lo, hi = pick(even, pair_ref, other_ref)
        has_lo = jnp.where(place[0] > 0, 1.0, 0.0)
        has_hi = jnp.where(place[0] + slab < place[1], 1.0, 0.0)
        estimate = mean_views(data_ref, views)
        level = level_of(estimate)
        ext = jnp.concatenate([lo - level * has_lo, estimate - level, hi - level * has_hi], axis=0)
        part = blur_back(0, views, slab, rows, level, data_ref, ext.astype(BF), mats, held)
        own_ref[0] = part[edge : edge + rows]
        put(even, part[0 : 2 * edge].astype(BF), part[rows:].astype(BF), to_pair, to_other)

    return kernel


def second_kernel(views, slab, rows, edge, lateral):
    scale = 1.0 / views

    def kernel(
        place, data_ref, pair0_ref, other0_ref, own_ref, sent_pair, sent_other, pair_ref, other_ref, w_ref, one_ref, *refs
    ):
        mats, (est_ref, part_ref, to_pair, to_other, held) = refs[:9], refs[9:]
        even = place[2] == 0
        has_lo = jnp.where(place[0] > 0, 1.0, 0.0)
        has_hi = jnp.where(place[0] + slab < place[1], 1.0, 0.0)
        lo, hi = pick(even, pair0_ref, other0_ref)
        got_lo, got_hi = pick(even, pair_ref, other_ref)
        sent_lo, sent_hi = pick(even, sent_pair, sent_other)
        lo = lo * (one_ref[0:edge] + scale * (sent_lo[0:edge] + got_lo[0:edge]))
        hi = hi * (one_ref[edge + rows :] + scale * (sent_hi[edge:] + got_hi[edge:]))
        got = jnp.concatenate([got_lo[edge:], got_hi[0:edge]], axis=0)
        before = mean_views(data_ref, views)
        level = level_of(before)
        estimate = before * (one_ref[pl.ds(edge, rows)] + scale * (own_ref[0] + got))
        est_ref[0] = estimate
        shape = across(w_ref[...], lateral) * level
        shapes = jnp.concatenate([shape] * (edge // shape.shape[0]), axis=0)
        ext = jnp.concatenate(
            [
                lo - shapes * has_lo,
                estimate - jnp.concatenate([shape] * slab, axis=0),
                hi - shapes * has_hi,
            ],
            axis=0,
        )
        part = blur_back(1, views, slab, rows, level, data_ref, ext.astype(BF), mats, held)
        part_ref[0] = part[edge : edge + rows]
        put(even, part[0:edge].astype(BF), part[edge + rows :].astype(BF), to_pair, to_other)

    return kernel


def table_kernel(slab, depth, lateral):
    half = lateral // 2

    def kernel(quarter_ref, wave_ref, _, waves_ref, back_ref, high_ref, low_ref):
        steps = [jnp.broadcast_to(quarter_ref[0:1, :], (8, 128)), jnp.broadcast_to(quarter_ref[1:2, :], (8, 128))]
        for j in range(half // 128):
            lane = iota((8, 128), 1) + j * 128
            phase = (iota((8, 128), 0) * lane) & (lateral - 1)
            for i in range(lateral // 16):
                pair = []
                for _ in range(2):
                    near, turn = phase & 127, phase // 128
                    g0 = jnp.take_along_axis(steps[0], near, axis=1)
                    g1 = jnp.take_along_axis(steps[1], near, axis=1)
                    odd = (turn & 1) == 1
                    cos = jnp.where(odd, g1, g0) * jnp.where(turn >= 2, -1.0, 1.0)
                    sin = jnp.where(odd, g0, g1) * jnp.where((turn == 0) | (turn == 3), -1.0, 1.0)
                    if j == 0:
                        flip = jnp.where((iota((8, 128), 0) & 1) == 1, -1.0, 1.0)
                        sin = jnp.where(lane == 0, flip, sin)
                    pair.append((cos, sin))
                    phase = (phase + lane * 8) & (lateral - 1)
                at = pl.ds(i * 16, 16)
                waves_ref[at, pl.ds(j * 128, 128)] = jnp.concatenate([pair[0][0], pair[1][0]], axis=0).astype(BF)
                waves_ref[at, pl.ds(half + j * 128, 128)] = jnp.concatenate(
                    [pair[0][1], pair[1][1]], axis=0
                ).astype(BF)
        for j in range(lateral // 128):
            lane = iota((8, 128), 1) + j * 128
            phase = (iota((8, 128), 0) * lane) & (lateral - 1)
            for i in range(half // 16):
                pair = []
                for s in range(2):
                    near, turn = phase & 127, phase // 128
                    g0 = jnp.take_along_axis(steps[0], near, axis=1)
                    g1 = jnp.take_along_axis(steps[1], near, axis=1)
                    odd = (turn & 1) == 1
                    cos = jnp.where(odd, g1, g0) * jnp.where(turn >= 2, -1.0, 1.0)
                    sin = jnp.where(odd, g0, g1) * jnp.where((turn == 0) | (turn == 3), 1.0, -1.0)
                    if i == 0 and s == 0:
                        flip = jnp.where((lane & 1) == 1, -1.0, 1.0)
                        sin = jnp.where(iota((8, 128), 0) == 0, flip, sin)
                    pair.append((cos, sin))
                    phase = (phase + lane * 8) & (lateral - 1)
                at = pl.ds(j * 128, 128)
                back_ref[pl.ds(i * 16, 16), at] = jnp.concatenate([pair[0][0], pair[1][0]], axis=0).astype(BF)
                back_ref[pl.ds(half + i * 16, 16), at] = jnp.concatenate([pair[0][1], pair[1][1]], axis=0).astype(BF)
        slot = iota((depth, 128), 1) // depth
        group = 128 // depth
        for kind in range(2):
            wave = wave_ref[kind]
            high = wave.astype(BF).astype(F32)
            for i in range(slab):
                for g in range(slab * depth // 128):
                    at = (pl.ds((kind * slab + i) * depth, depth), pl.ds(g * 128, 128))
                    here = slot == i - group * g
                    high_ref[at] = jnp.where(here, high, 0.0).astype(BF)
                    low_ref[at] = jnp.where(here, wave - high, 0.0).astype(BF)

    return kernel


def split_dot(table_hi, table_lo, x):
    x_hi = x.astype(BF)
    x_lo = (x - x_hi.astype(F32)).astype(BF)
    return dot(table_hi, x_hi) + dot(table_hi, x_lo) + dot(table_lo, x_hi)


def spectrum(even, scale, rows, half, est_ref, part_ref, pair_ref, other_ref, one_ref, waves_ref, high_ref, low_ref):
    got_lo, got_hi = pick(even, pair_ref, other_ref)
    got = jnp.concatenate([got_lo, got_hi], axis=0)
    estimate = est_ref[0] * (one_ref[...] + scale * (part_ref[0] + got))
    row = dot(estimate.astype(BF), waves_ref[...])
    from_cos = split_dot(high_ref[...], low_ref[...], row[:, :half])
    from_sin = split_dot(high_ref[...], low_ref[...], row[:, half:])
    first = iota((rows, half), 1) == 0
    sin_cos = from_sin[:rows]
    sin_sin = from_sin[rows:]
    real = from_cos[:rows] - jnp.where(first, 0.0, sin_sin)
    imag = -from_cos[rows:] - jnp.where(first, 0.0, sin_cos)
    top = iota((rows, 128), 1) == 0
    top_real = jnp.where(top, sin_cos[:, :128], 0.0)
    top_imag = jnp.where(top, -sin_sin[:, :128], 0.0)
    return real, imag, top_real, top_imag


def spectrum_kernel(views, slab, depth, lateral):
    rows, half = slab * depth, lateral // 2

    def kernel(place, est_ref, part_ref, pair_ref, other_ref, one_ref, waves_ref, high_ref, low_ref, *outs):
        even = place[2] == 0
        args = (est_ref, part_ref, pair_ref, other_ref, one_ref, waves_ref, high_ref, low_ref)
        for ref, value in zip(outs, spectrum(even, 1.0 / views, rows, half, *args)):
            ref[...] = value

    return kernel


def power_kernel(views, slab, depth, lateral, count):
    rows, half = slab * depth, lateral // 2

    def kernel(
        place,
        est_ref,
        part_ref,
        pair_ref,
        other_ref,
        one_ref,
        waves_ref,
        high_ref,
        low_ref,
        map_ref,
        re_ref,
        im_ref,
        tre_ref,
        tim_ref,
        mre_ref,
        mim_ref,
        mtre_ref,
        mtim_ref,
        sum_ref,
    ):
        even = place[2] == 0
        args = (est_ref, part_ref, pair_ref, other_ref, one_ref, waves_ref, high_ref, low_ref)
        re1, im1, tre1, tim1 = spectrum(even, 1.0 / views, rows, half, *args)
        re0, im0, tre0, tim0 = re_ref[...], im_ref[...], tre_ref[...], tim_ref[...]
        mre_ref[...] = 0.5 * (re0 + re1)
        mim_ref[...] = 0.5 * (im0 + im1)
        mtre_ref[...] = 0.5 * (tre0 + tre1)
        mtim_ref[...] = 0.5 * (tim0 + tim1)

        def over_slab(x):
            total = x[0:depth]
            for s in range(1, slab):
                total = total + x[s * depth : (s + 1) * depth]
            return total

        twice = jnp.where(iota((depth, half), 1) == 0, 1.0, 2.0)
        powers, tops = [], []
        for a, b, c, d in (
            (re0, re1, im0, im1),
            (re0, re0, im0, im0),
            (re1, re1, im1, im1),
        ):
            powers.append(over_slab(a * b + c * d) * twice)
        for a, b, c, d in (
            (tre0, tre1, tim0, tim1),
            (tre0, tre0, tim0, tim0),
            (tre1, tre1, tim1, tim1),
        ):
            tops.append(jnp.sum(over_slab(a * b + c * d), axis=0, keepdims=True))
        top = jnp.sum(jnp.concatenate(tops, axis=0), axis=1, keepdims=True)
        total = jnp.zeros((9, CYCLES), F32)
        cycle = iota((CYCLES, half), 0)
        for k in range(depth // 2 + 1):
            other = depth - k
            terms = [p[k : k + 1] + p[other : other + 1] if 0 < k < other else p[k : k + 1] for p in powers]
            term = jnp.concatenate(terms, axis=0)
            high = term.astype(BF).astype(F32)
            middle = (term - high).astype(BF).astype(F32)
            low = term - high - middle
            term = jnp.concatenate([high, middle, low], axis=0).astype(BF)
            onehot = (map_ref[0, k : k + 1, 0:half] == cycle).astype(F32).astype(BF)
            total = total + lax.dot_general(
                term, onehot, (((1,), (1,)), ((), ())), preferred_element_type=F32
            )
        last = jnp.where(iota((3, CYCLES), 1) == CYCLES - 1, top, 0.0)
        total = total[0:3] + total[3:6] + total[6:9] + last
        for i in range(count):
            sum_ref[i] = total

    return kernel


def inverse_kernel(slab, depth, lateral, count):
    rows, half = slab * depth, lateral // 2

    def kernel(cut_ref, sum_ref, map_ref, mre_ref, mim_ref, mtre_ref, mtim_ref, back_ref, high_ref, low_ref, out_ref):
        total = sum_ref[0]
        for i in range(1, count):
            total = total + sum_ref[i]
        cross, power0, power1 = total[0:1], total[1:2], total[2:3]
        corr = cross / (jnp.sqrt(power0) * jnp.sqrt(power1))
        weight = jnp.where(iota((1, CYCLES), 1) <= cut_ref[0], corr, 0.0)
        low = jnp.broadcast_to(weight[:, 0:128], (depth, 128))
        high = jnp.broadcast_to(weight[:, 128:256], (depth, 128))
        pieces = []
        for j in range(half // 128):
            cell = map_ref[0, :, pl.ds(j * 128, 128)]
            near = cell & 127
            found = jnp.where(
                cell < 128,
                jnp.take_along_axis(low, near, axis=1),
                jnp.take_along_axis(high, near, axis=1),
            )
            twice = jnp.where(iota((depth, 128), 1) + j * 128 == 0, 1.0, 2.0)
            pieces.append(found * twice)
        cells = jnp.concatenate(pieces, axis=1)
        cells = jnp.concatenate([cells] * slab, axis=0)
        last = weight[:, CYCLES - 1 : CYCLES]
        re = mre_ref[...] * cells
        im = mim_ref[...] * cells
        re = jnp.concatenate([re[:, :128] - mtim_ref[...] * last, re[:, 128:]], axis=1)
        im = jnp.concatenate([im[:, :128] + mtre_ref[...] * last, im[:, 128:]], axis=1)
        from_re = split_dot(high_ref[...], low_ref[...], re)
        from_im = split_dot(high_ref[...], low_ref[...], im)
        inner_re = (from_re[:rows] - from_im[rows:]).astype(BF)
        inner_im = (from_re[rows:] + from_im[:rows]).astype(BF)
        joined = dot(inner_re, back_ref[0:half]) + dot(inner_im, back_ref[half:lateral])
        out_ref[...] = joined * (1.0 / (depth * lateral))

    return kernel


def body(data_halves, psf_taps, cycle_map, cutoff):
    _, views, slab, depth, lateral = data_halves.shape
    taps = psf_taps.shape[-1]
    radius = taps // 2
    rows, edge = slab * depth, radius * depth
    ext_rows = rows + 2 * edge
    half = lateral // 2
    count = lax.axis_size("tile")
    index = lax.axis_index("tile")
    pairs = [(i, i ^ 1) for i in range(count)]
    others = [(i, i + 1) for i in range(1, count - 1, 2)]
    others = others + [(b, a) for a, b in others]

    def exchange(to_pair, to_other):
        other = lax.ppermute(to_other, "tile", others)
        return lax.ppermute(to_pair, "tile", pairs), other

    def whole(array):
        return pl.BlockSpec(array.shape, lambda i: (0,) * len(array.shape))

    def half_of(array, h, size=None, at=0):
        shape = (1,) + array.shape[1:] if size is None else (1, size) + array.shape[2:]
        return pl.BlockSpec(shape, lambda i: (h, at) + (0,) * (len(shape) - 2))

    def call(kernel, inputs, outputs, name, scratch=(), flops=0):
        arrays = [x[0] if isinstance(x, tuple) else x for x in inputs]
        specs = []
        for x in inputs:
            if isinstance(x, tuple):
                specs.append(x[1])
            else:
                specs.append(whole(x))
        bytes_moved = sum(int(np.prod(s.shape)) * s.dtype.itemsize for s in outputs)
        return pl.pallas_call(
            kernel,
            grid=(1,),
            in_specs=specs,
            out_specs=tuple(whole(s) for s in outputs),
            out_shape=tuple(outputs),
            scratch_shapes=list(scratch),
            cost_estimate=pl.CostEstimate(flops=flops, bytes_accessed=2 * bytes_moved, transcendentals=0),
            compiler_params=pltpu.CompilerParams(vmem_limit_bytes=VMEM_LIMIT),
            name=name,
        )(*arrays)

    def shaped(*shape, dtype=F32):
        return jax.ShapeDtypeStruct(shape, dtype)

    scalars = pl.BlockSpec(memory_space=pltpu.SMEM)
    data = data_halves.reshape(2, views, rows, lateral)
    start = jnp.mean(data.astype(F32), axis=1).astype(BF)
    even = index % 2 == 0
    low, high = start[:, :edge], start[:, rows - edge :]
    pair0, other0 = exchange(jnp.where(even, high, low), jnp.where(even, low, high))

    kernels = psf_taps / jnp.sum(psf_taps, axis=-1, keepdims=True)
    place = (jnp.stack([index * slab, jnp.int32(count * slab), index % 2]), scalars)
    band = shaped(views, 256, 256, dtype=BF)
    *mats, shape, one0, one1 = call(
        prep_kernel(views, taps, slab, depth, lateral),
        [(kernels.reshape(-1), scalars), place],
        [
            shaped(views * rows, ext_rows, dtype=BF),
            shaped(ext_rows, views * rows, dtype=BF),
            band,
            band,
            band,
            band,
            shaped(2, views * rows, 128),
            shaped(2, views, depth, 128),
            shaped(views, 2, 8, lateral),
            shaped(depth, 128),
            shaped(ext_rows, lateral),
            shaped(rows, lateral),
        ],
        "prep",
        flops=4 * 10**9,
    )

    held = [pltpu.VMEM((views * rows, lateral), BF)]
    firsts = []
    for h in range(2):
        own, to_pair, to_other = call(
            first_kernel(views, slab, rows, edge),
            [place, (data, half_of(data, h)), (pair0, half_of(pair0, h)), (other0, half_of(other0, h))] + mats,
            [shaped(1, rows, lateral)] + [shaped(1, 2 * edge, lateral, dtype=BF)] * 2,
            f"first{h}",
            held,
            flops=4 * 10**9,
        )
        firsts.append((own, to_pair, to_other) + exchange(to_pair, to_other))

    angle = 2.0 * np.pi / lateral * np.arange(256)
    quarter = jnp.asarray(np.cos(angle).astype(np.float32).reshape(2, 128))
    grid_z = np.arange(depth)[:, None] * np.arange(depth)[None, :] % depth * (2.0 * np.pi / depth)
    wave = np.stack([np.cos(grid_z), np.sin(grid_z)]).astype(np.float32)
    wave = jnp.asarray(np.tile(wave, (1, 1, 128 // depth)))
    table = shaped(2 * rows, rows, dtype=BF)
    waves, back, table_hi, table_lo = call(
        table_kernel(slab, depth, lateral),
        [quarter, wave, (firsts[1][0], pl.BlockSpec((1, 8, 128), lambda i: (0, 0, 0)))],
        [shaped(lateral, lateral, dtype=BF), shaped(lateral, lateral, dtype=BF), table, table],
        "tables",
        flops=2 * 10**9,
    )

    seconds = []
    for h in range(2):
        own, to_pair, to_other, pair, other = firsts[h]
        est, part, to_pair, to_other = call(
            second_kernel(views, slab, rows, edge, lateral),
            [place, (data, half_of(data, h)), (pair0, half_of(pair0, h)), (other0, half_of(other0, h))]
            + [own, to_pair, to_other, pair, other, shape, one0]
            + mats,
            [shaped(1, rows, lateral)] * 2 + [shaped(1, edge, lateral, dtype=BF)] * 2,
            f"second{h}",
            held,
            flops=4 * 10**9,
        )
        seconds.append((est, part) + exchange(to_pair, to_other))

    plane, top = shaped(rows, half), shaped(rows, 128)
    tables = [one1, waves, table_hi, table_lo]
    spectra = call(
        spectrum_kernel(views, slab, depth, lateral),
        [place, *seconds[0]] + tables,
        [plane, plane, top, top],
        "spectrum0",
        flops=10**9,
    )
    *mixed, sums = call(
        power_kernel(views, slab, depth, lateral, count),
        [place, *seconds[1]] + tables + [cycle_map, *spectra],
        [plane, plane, top, top, shaped(count, 3, CYCLES)],
        "spectrum1",
        flops=2 * 10**9,
    )
    sums = lax.all_to_all(sums, "tile", 0, 0)
    (joined,) = call(
        inverse_kernel(slab, depth, lateral, count),
        [(cutoff, scalars), sums, cycle_map, *mixed, back, table_hi, table_lo],
        [shaped(rows, lateral)],
        "inverse",
        flops=10**9,
    )
    return joined.reshape(slab, depth, lateral)


def solution(mesh):
    in_specs = (
        P(None, None, ("groups", "tile"), None, None),
        P(),
        P(("groups", "tile"), None, None),
        P("groups"),
    )
    out_specs = P(("groups", "tile"), None, None)
    return jax.shard_map(body, mesh=mesh, in_specs=in_specs, out_specs=out_specs, check_vma=False)
```

```python
import jax
import jax.numpy as jnp
import numpy as np
from jax import lax
from jax.experimental import pallas as pl
from jax.experimental.pallas import tpu as pltpu
from jax.sharding import PartitionSpec as P

CYCLES = 256
BF = jnp.bfloat16
F32 = jnp.float32
VMEM_LIMIT = 32 * 1024 * 1024


def dot(a, b):
    return lax.dot_general(a, b, (((1,), (0,)), ((), ())), preferred_element_type=F32)


def iota(shape, dim):
    return lax.broadcasted_iota(jnp.int32, shape, dim)


def lookup(index, values):
    total = jnp.zeros(index.shape, F32)
    for place, value in values:
        total = jnp.where(index == place, value, total)
    return total


def shift_rows(x, by):
    count = x.shape[0]
    if by == 0:
        return x
    pad = jnp.zeros((abs(by), x.shape[1]), x.dtype)
    if by > 0:
        return jnp.concatenate([x[by:], pad], axis=0)
    return jnp.concatenate([pad, x[: count + by]], axis=0)


def prep_kernel(views, taps, slab, depth, lateral):
    radius = taps // 2
    group = 128 // depth
    ext = slab + 2 * radius
    rows = slab * depth
    scale = 1.0 / views

    def kernel(kern, a_ref, b_ref, t_ref, tt_ref, base_ref, off_ref, row_ref, w_ref, one0_ref, one1_ref):
        first = lax.axis_index("tile") * slab
        rows_total = lax.axis_size("tile") * slab

        def tap(v, axis, t):
            return kern[(v * 3 + axis) * taps + t]

        def ones(v, axis, index, count, flip):
            summed = jnp.zeros(index.shape, F32)
            for t in range(taps):
                source = index + t - radius
                ok = (source >= 0) & (source < count)
                summed = summed + jnp.where(ok, tap(v, axis, taps - 1 - t if flip else t), 0.0)
            return summed

        row = iota((depth, 128), 0)
        lane = iota((depth, 128), 1)
        cell = lax.rem(lane, depth)
        slot = lane // depth
        gap_z = cell - row + radius
        gap_zt = row - cell + radius
        gap = iota((128, 128), 0) - iota((128, 128), 1) + radius
        upper_gap = gap[120:128] - 128
        lower_gap = gap[0:8] + 128
        zero = jnp.zeros((depth, 128), BF)
        tail = jnp.zeros((120, 128), F32)
        gains = []
        for v in range(views):
            band_z = lookup(gap_z, [(t, tap(v, 1, t)) for t in range(taps)])
            band_zt = lookup(gap_zt, [(t, tap(v, 1, t)) for t in range(taps)])

            def lane_taps(shift, sign, v=v):
                pairs = [(j, shift + sign * j) for j in range(group)]
                pairs = [(j, tap(v, 0, t)) for j, t in pairs if 0 <= t < taps]
                return lookup(slot, pairs) if pairs else None

            blocks = {}
            for i in range(slab):
                for g in range(ext * depth // 128):
                    d = group * g - i
                    if d not in blocks:
                        weight = lane_taps(d, 1)
                        blocks[d] = zero if weight is None else (weight * band_z).astype(BF)
                    a_ref[pl.ds((v * slab + i) * depth, depth), pl.ds(g * 128, 128)] = blocks[d]
            blocks = {}
            for i in range(ext):
                for g in range(rows // 128):
                    d = i - group * g
                    if d not in blocks:
                        weight = lane_taps(d, -1)
                        blocks[d] = zero if weight is None else (weight * band_zt).astype(BF)
                    b_ref[pl.ds(i * depth, depth), pl.ds(v * rows + g * 128, 128)] = blocks[d]

            for flip, band_ref in ((False, t_ref), (True, tt_ref)):
                pairs = [(t, tap(v, 2, taps - 1 - t if flip else t)) for t in range(taps)]
                middle = lookup(gap, pairs).astype(BF)
                upper = jnp.concatenate([tail, lookup(upper_gap, pairs[:radius])], axis=0).astype(BF)
                lower = jnp.concatenate([lookup(lower_gap, pairs[radius + 1 :]), tail], axis=0).astype(BF)
                for at, block in ((0, middle), (1, upper), (2, lower), (3, middle)):
                    at_rows, at_cols = pl.ds(at // 2 * 128, 128), pl.ds(at % 2 * 128, 128)
                    band_ref[v, at_rows, at_cols] = block

            mid = depth // 2
            sum_xz = jnp.sum(
                a_ref[pl.ds(v * rows, depth), :].astype(F32)[mid : mid + 1], axis=1, keepdims=True
            )
            sum_y = jnp.sum(t_ref[v, 0:128, :].astype(F32)[64:65], axis=1, keepdims=True)
            gains.append(1.0 / (sum_xz * sum_y))

        def blur_z(v, x, flip):
            total = None
            for t in range(taps):
                term = shift_rows(x, t - radius) * tap(v, 1, taps - 1 - t if flip else t)
                total = term if total is None else total + term
            return total

        field0 = [ones(v, 1, row, depth, False) for v in range(views)]
        back0 = [blur_z(v, 1.0 / field0[v], True) for v in range(views)]
        shape = back0[0]
        for v in range(1, views):
            shape = shape + back0[v]
        shape = shape * scale
        w_ref[...] = shape
        field1 = [blur_z(v, shape, False) for v in range(views)]
        back1 = [blur_z(v, 1.0 / field1[v], True) for v in range(views)]

        x_out = iota((slab, 128), 0) + first
        x_ext = iota((ext, 128), 0) + (first - radius)
        y_row = iota((8, lateral), 1)
        edges = []
        for v in range(views):
            part_x = ones(v, 0, x_out, rows_total, False)
            for n, field in enumerate((field0, field1)):
                for i in range(slab):
                    at = pl.ds((v * slab + i) * depth, depth)
                    base_ref[n, at, :] = field[v] * part_x[i : i + 1]
                off_ref[n, v] = gains[v] / field[v]
            row_ref[v, 0] = ones(v, 2, y_row, lateral, False)
            row_ref[v, 1] = jnp.broadcast_to(gains[v], (8, lateral))
            edges.append((ones(v, 0, x_ext, rows_total, True) * scale, ones(v, 2, y_row, lateral, True)))
        for n, back, one_ref, low, high in (
            (0, back0, one0_ref, 0, ext),
            (1, back1, one1_ref, radius, radius + slab),
        ):
            for e in range(low, high):
                terms = [back[v] * edges[v][0][e : e + 1] for v in range(views)]
                for j in range(lateral // 128):
                    total = None
                    for v in range(views):
                        term = terms[v]
                        if j in (0, lateral // 128 - 1):
                            term = term * edges[v][1][0:1, j * 128 : (j + 1) * 128]
                        total = term if total is None else total + term
                    one_ref[pl.ds((e - low) * depth, depth), pl.ds(j * 128, 128)] = total

    return kernel


def y_blur(x, band):
    rows = x.shape[0]
    stacked = jnp.concatenate([x[:, 0:256], x[:, 128:384], x[:, 256:512]], axis=0)
    wide = dot(stacked, band)
    left, mid, right = wide[:rows], wide[rows : 2 * rows], wide[2 * rows :]
    low = iota((rows, 128), 1) < 64
    return jnp.concatenate(
        [
            left[:, :128],
            jnp.where(low, left[:, 128:], mid[:, :128]),
            jnp.where(low, mid[:, 128:], right[:, :128]),
            right[:, 128:],
        ],
        axis=1,
    )


def mean_views(h, data_ref, views):
    total = data_ref[h, 0].astype(F32)
    for v in range(1, views):
        total = total + data_ref[h, v].astype(F32)
    return total * (1.0 / views)


def level_of(x):
    total = jnp.sum(jnp.sum(x, axis=0, keepdims=True), axis=1, keepdims=True)
    return (total * (1.0 / x.size)).astype(BF).astype(F32)


def across(x, lateral):
    return jnp.concatenate([x] * (lateral // 128), axis=1)


def blur_back(n, h, views, slab, rows, level, data_ref, ext, mats, held):
    a_ref, b_ref, t_ref, tt_ref, base_ref, off_ref, row_ref = mats
    lateral = ext.shape[1]
    held[...] = dot(a_ref[...], ext).astype(BF)
    for v in range(views):
        part = held[pl.ds(v * rows, rows), :]
        base = across(base_ref[n, pl.ds(v * rows, rows), :], lateral) * (row_ref[v, 0, 0:1, :] * level)
        predicted = y_blur(part, t_ref[v]) + base
        scaled = data_ref[h, v].astype(F32) * row_ref[v, 1, 0:1, :]
        offset = across(jnp.concatenate([off_ref[n, v]] * slab, axis=0), lateral)
        quotient = (scaled / predicted - offset).astype(BF)
        held[pl.ds(v * rows, rows), :] = y_blur(quotient, tt_ref[v]).astype(BF)
    return dot(b_ref[...], held[...])


def pick(even, from_pair, from_other, h=0):
    pair = from_pair[h].astype(F32)
    other = from_other[h].astype(F32)
    return jnp.where(even, other, pair), jnp.where(even, pair, other)


def put(even, low, high, to_pair, to_other, h=0):
    @pl.when(even)
    def _():
        to_pair[h] = high
        to_other[h] = low

    @pl.when(jnp.logical_not(even))
    def _():
        to_pair[h] = low
        to_other[h] = high


def is_even():
    return (lax.axis_index("tile") & 1) == 0


def has_sides():
    index = lax.axis_index("tile")
    return jnp.where(index > 0, 1.0, 0.0), jnp.where(index + 1 < lax.axis_size("tile"), 1.0, 0.0)


def edge_kernel(views, rows, edge):
    def kernel(data_hbm, data_ref, to_pair, to_other, sems):
        copies = {}
        for h in range(2):
            for v in range(views):
                copies[h, v] = pltpu.make_async_copy(
                    data_hbm.at[h, v], data_ref.at[h, v], sems.at[h * views + v]
                )
                copies[h, v].start()
        even = is_even()
        for h in range(2):
            for v in range(views):
                copies[h, v].wait()
            start = mean_views(h, data_ref, views).astype(BF)
            put(even, start[:edge], start[rows - edge :], to_pair, to_other, h)

    return kernel


def first_kernel(h, views, slab, rows, edge):
    def kernel(data_ref, pair_ref, other_ref, *refs):
        mats, (own_ref, to_pair, to_other, held) = refs[:7], refs[7:]
        even = is_even()
        lo, hi = pick(even, pair_ref, other_ref, h)
        has_lo, has_hi = has_sides()
        estimate = mean_views(h, data_ref, views)
        level = level_of(estimate)
        ext = jnp.concatenate([lo - level * has_lo, estimate - level, hi - level * has_hi], axis=0)
        part = blur_back(0, h, views, slab, rows, level, data_ref, ext.astype(BF), mats, held)
        own_ref[0] = part[edge : edge + rows]
        put(even, part[0 : 2 * edge].astype(BF), part[rows:].astype(BF), to_pair, to_other)

    return kernel


def second_kernel(h, views, slab, rows, edge, lateral):
    scale = 1.0 / views

    def kernel(
        data_ref, pair0_ref, other0_ref, own_ref, sent_pair, sent_other, pair_ref, other_ref, w_ref, one_ref, *refs
    ):
        mats, (est_ref, part_ref, to_pair, to_other, held) = refs[:7], refs[7:]
        even = is_even()
        has_lo, has_hi = has_sides()
        lo, hi = pick(even, pair0_ref, other0_ref, h)
        got_lo, got_hi = pick(even, pair_ref, other_ref)
        sent_lo, sent_hi = pick(even, sent_pair, sent_other)
        lo = lo * (one_ref[0:edge] + scale * (sent_lo[0:edge] + got_lo[0:edge]))
        hi = hi * (one_ref[edge + rows :] + scale * (sent_hi[edge:] + got_hi[edge:]))
        got = jnp.concatenate([got_lo[edge:], got_hi[0:edge]], axis=0)
        before = mean_views(h, data_ref, views)
        level = level_of(before)
        estimate = before * (one_ref[pl.ds(edge, rows)] + scale * (own_ref[0] + got))
        est_ref[0] = estimate
        shape = across(w_ref[...], lateral) * level
        shapes = jnp.concatenate([shape] * (edge // shape.shape[0]), axis=0)
        ext = jnp.concatenate(
            [
                lo - shapes * has_lo,
                estimate - jnp.concatenate([shape] * slab, axis=0),
                hi - shapes * has_hi,
            ],
            axis=0,
        )
        part = blur_back(1, h, views, slab, rows, level, data_ref, ext.astype(BF), mats, held)
        part_ref[0] = part[edge : edge + rows]
        put(even, part[0:edge].astype(BF), part[edge + rows :].astype(BF), to_pair, to_other)

    return kernel


def table_kernel(slab, depth, lateral):
    half = lateral // 2

    def kernel(quarter_ref, wave_ref, _, waves_ref, back_ref, high_ref, low_ref):
        steps = [jnp.broadcast_to(quarter_ref[0:1, :], (8, 128)), jnp.broadcast_to(quarter_ref[1:2, :], (8, 128))]
        for j in range(half // 128):
            lane = iota((8, 128), 1) + j * 128
            phase = (iota((8, 128), 0) * lane) & (lateral - 1)
            for i in range(lateral // 16):
                pair = []
                for _ in range(2):
                    near, turn = phase & 127, phase // 128
                    g0 = jnp.take_along_axis(steps[0], near, axis=1)
                    g1 = jnp.take_along_axis(steps[1], near, axis=1)
                    odd = (turn & 1) == 1
                    cos = jnp.where(odd, g1, g0) * jnp.where(turn >= 2, -1.0, 1.0)
                    sin = jnp.where(odd, g0, g1) * jnp.where((turn == 0) | (turn == 3), -1.0, 1.0)
                    if j == 0:
                        flip = jnp.where((iota((8, 128), 0) & 1) == 1, -1.0, 1.0)
                        sin = jnp.where(lane == 0, flip, sin)
                    pair.append((cos, sin))
                    phase = (phase + lane * 8) & (lateral - 1)
                at = pl.ds(i * 16, 16)
                waves_ref[at, pl.ds(j * 128, 128)] = jnp.concatenate([pair[0][0], pair[1][0]], axis=0).astype(BF)
                waves_ref[at, pl.ds(half + j * 128, 128)] = jnp.concatenate(
                    [pair[0][1], pair[1][1]], axis=0
                ).astype(BF)
        for j in range(lateral // 128):
            lane = iota((8, 128), 1) + j * 128
            phase = (iota((8, 128), 0) * lane) & (lateral - 1)
            for i in range(half // 16):
                pair = []
                for s in range(2):
                    near, turn = phase & 127, phase // 128
                    g0 = jnp.take_along_axis(steps[0], near, axis=1)
                    g1 = jnp.take_along_axis(steps[1], near, axis=1)
                    odd = (turn & 1) == 1
                    cos = jnp.where(odd, g1, g0) * jnp.where(turn >= 2, -1.0, 1.0)
                    sin = jnp.where(odd, g0, g1) * jnp.where((turn == 0) | (turn == 3), 1.0, -1.0)
                    if i == 0 and s == 0:
                        flip = jnp.where((lane & 1) == 1, -1.0, 1.0)
                        sin = jnp.where(iota((8, 128), 0) == 0, flip, sin)
                    pair.append((cos, sin))
                    phase = (phase + lane * 8) & (lateral - 1)
                at = pl.ds(j * 128, 128)
                back_ref[pl.ds(i * 16, 16), at] = jnp.concatenate([pair[0][0], pair[1][0]], axis=0).astype(BF)
                back_ref[pl.ds(half + i * 16, 16), at] = jnp.concatenate([pair[0][1], pair[1][1]], axis=0).astype(BF)
        slot = iota((depth, 128), 1) // depth
        group = 128 // depth
        for kind in range(2):
            wave = wave_ref[kind]
            high = wave.astype(BF).astype(F32)
            for i in range(slab):
                for g in range(slab * depth // 128):
                    at = (pl.ds((kind * slab + i) * depth, depth), pl.ds(g * 128, 128))
                    here = slot == i - group * g
                    high_ref[at] = jnp.where(here, high, 0.0).astype(BF)
                    low_ref[at] = jnp.where(here, wave - high, 0.0).astype(BF)

    return kernel


def split_dot(table_hi, table_lo, x):
    x_hi = x.astype(BF)
    x_lo = (x - x_hi.astype(F32)).astype(BF)
    return dot(table_hi, x_hi) + dot(table_hi, x_lo) + dot(table_lo, x_hi)


def spectrum(even, scale, rows, half, est_ref, part_ref, pair_ref, other_ref, one_ref, waves_ref, high_ref, low_ref):
    got_lo, got_hi = pick(even, pair_ref, other_ref)
    got = jnp.concatenate([got_lo, got_hi], axis=0)
    estimate = est_ref[0] * (one_ref[...] + scale * (part_ref[0] + got))
    row = dot(estimate.astype(BF), waves_ref[...])
    from_cos = split_dot(high_ref[...], low_ref[...], row[:, :half])
    from_sin = split_dot(high_ref[...], low_ref[...], row[:, half:])
    first = iota((rows, half), 1) == 0
    sin_cos = from_sin[:rows]
    sin_sin = from_sin[rows:]
    real = from_cos[:rows] - jnp.where(first, 0.0, sin_sin)
    imag = -from_cos[rows:] - jnp.where(first, 0.0, sin_cos)
    top = iota((rows, 128), 1) == 0
    top_real = jnp.where(top, sin_cos[:, :128], 0.0)
    top_imag = jnp.where(top, -sin_sin[:, :128], 0.0)
    return real, imag, top_real, top_imag


def spectrum_kernel(views, slab, depth, lateral):
    rows, half = slab * depth, lateral // 2

    def kernel(est_ref, part_ref, pair_ref, other_ref, one_ref, waves_ref, high_ref, low_ref, *outs):
        even = is_even()
        args = (est_ref, part_ref, pair_ref, other_ref, one_ref, waves_ref, high_ref, low_ref)
        for ref, value in zip(outs, spectrum(even, 1.0 / views, rows, half, *args)):
            ref[...] = value

    return kernel


def cycle_kernel(depth, half):
    def kernel(map_ref, cycle_ref):
        columns = jnp.transpose(map_ref[0, :, 0:half].astype(F32))
        cycle = iota((half, CYCLES), 1).astype(F32)
        for k in range(depth // 2 + 1):
            here = columns[:, k : k + 1] == cycle
            cycle_ref[pl.ds(k * half, half), :] = jnp.where(here, 1.0, 0.0).astype(BF)

    return kernel


def power_kernel(views, slab, depth, lateral, count):
    rows, half = slab * depth, lateral // 2

    def kernel(
        est_ref,
        part_ref,
        pair_ref,
        other_ref,
        one_ref,
        waves_ref,
        high_ref,
        low_ref,
        cycle_ref,
        re_ref,
        im_ref,
        tre_ref,
        tim_ref,
        mre_ref,
        mim_ref,
        mtre_ref,
        mtim_ref,
        sum_ref,
    ):
        even = is_even()
        args = (est_ref, part_ref, pair_ref, other_ref, one_ref, waves_ref, high_ref, low_ref)
        re1, im1, tre1, tim1 = spectrum(even, 1.0 / views, rows, half, *args)
        re0, im0, tre0, tim0 = re_ref[...], im_ref[...], tre_ref[...], tim_ref[...]
        mre_ref[...] = 0.5 * (re0 + re1)
        mim_ref[...] = 0.5 * (im0 + im1)
        mtre_ref[...] = 0.5 * (tre0 + tre1)
        mtim_ref[...] = 0.5 * (tim0 + tim1)

        def over_slab(x):
            total = x[0:depth]
            for s in range(1, slab):
                total = total + x[s * depth : (s + 1) * depth]
            return total

        twice = jnp.where(iota((depth, half), 1) == 0, 1.0, 2.0)
        powers, tops = [], []
        for a, b, c, d in (
            (re0, re1, im0, im1),
            (re0, re0, im0, im0),
            (re1, re1, im1, im1),
        ):
            powers.append(over_slab(a * b + c * d) * twice)
        for a, b, c, d in (
            (tre0, tre1, tim0, tim1),
            (tre0, tre0, tim0, tim0),
            (tre1, tre1, tim1, tim1),
        ):
            tops.append(jnp.sum(over_slab(a * b + c * d), axis=0, keepdims=True))
        top = jnp.sum(jnp.concatenate(tops, axis=0), axis=1, keepdims=True)
        terms = []
        for k in range(depth // 2 + 1):
            other = depth - k
            fold = [p[k : k + 1] + p[other : other + 1] if 0 < k < other else p[k : k + 1] for p in powers]
            terms.append(jnp.concatenate(fold, axis=0))
        term = jnp.concatenate(terms, axis=1)
        high = term.astype(BF).astype(F32)
        middle = (term - high).astype(BF).astype(F32)
        low = term - high - middle
        total = dot(jnp.concatenate([high, middle, low], axis=0).astype(BF), cycle_ref[...])
        last = jnp.where(iota((3, CYCLES), 1) == CYCLES - 1, top, 0.0)
        total = total[0:3] + total[3:6] + total[6:9] + last
        for i in range(count):
            sum_ref[i] = total

    return kernel


def inverse_kernel(slab, depth, lateral, count):
    rows, half = slab * depth, lateral // 2

    def kernel(cut_ref, sum_ref, map_ref, mre_ref, mim_ref, mtre_ref, mtim_ref, back_ref, high_ref, low_ref, out_ref):
        total = sum_ref[0]
        for i in range(1, count):
            total = total + sum_ref[i]
        cross, power0, power1 = total[0:1], total[1:2], total[2:3]
        corr = cross / (jnp.sqrt(power0) * jnp.sqrt(power1))
        weight = jnp.where(iota((1, CYCLES), 1) <= cut_ref[0], corr, 0.0)
        low = jnp.broadcast_to(weight[:, 0:128], (depth, 128))
        high = jnp.broadcast_to(weight[:, 128:256], (depth, 128))
        pieces = []
        for j in range(half // 128):
            cell = map_ref[0, :, pl.ds(j * 128, 128)]
            near = cell & 127
            found = jnp.where(
                cell < 128,
                jnp.take_along_axis(low, near, axis=1),
                jnp.take_along_axis(high, near, axis=1),
            )
            twice = jnp.where(iota((depth, 128), 1) + j * 128 == 0, 1.0, 2.0)
            pieces.append(found * twice)
        cells = jnp.concatenate(pieces, axis=1)
        cells = jnp.concatenate([cells] * slab, axis=0)
        last = weight[:, CYCLES - 1 : CYCLES]
        re = mre_ref[...] * cells
        im = mim_ref[...] * cells
        re = jnp.concatenate([re[:, :128] - mtim_ref[...] * last, re[:, 128:]], axis=1)
        im = jnp.concatenate([im[:, :128] + mtre_ref[...] * last, im[:, 128:]], axis=1)
        from_re = split_dot(high_ref[...], low_ref[...], re)
        from_im = split_dot(high_ref[...], low_ref[...], im)
        inner_re = (from_re[:rows] - from_im[rows:]).astype(BF)
        inner_im = (from_re[rows:] + from_im[:rows]).astype(BF)
        joined = dot(inner_re, back_ref[0:half]) + dot(inner_im, back_ref[half:lateral])
        out_ref[...] = joined * (1.0 / (depth * lateral))

    return kernel


def body(data_halves, psf_taps, cycle_map, cutoff):
    _, views, slab, depth, lateral = data_halves.shape
    taps = psf_taps.shape[-1]
    radius = taps // 2
    rows, edge = slab * depth, radius * depth
    ext_rows = rows + 2 * edge
    half = lateral // 2
    count = lax.axis_size("tile")
    pairs = [(i, i ^ 1) for i in range(count)]
    others = [(i, i + 1) for i in range(1, count - 1, 2)]
    others = others + [(b, a) for a, b in others]

    def exchange(to_pair, to_other):
        other = lax.ppermute(to_other, "tile", others)
        return lax.ppermute(to_pair, "tile", pairs), other

    vmem = pl.BlockSpec(memory_space=pltpu.VMEM)
    scalars = pl.BlockSpec(memory_space=pltpu.SMEM)

    def call(kernel, inputs, outputs, name, scratch=(), flops=0):
        bytes_moved = sum(int(np.prod(s.shape)) * s.dtype.itemsize for s in outputs)
        return pl.pallas_call(
            kernel,
            in_specs=[scalars if isinstance(x, tuple) else vmem for x in inputs],
            out_specs=tuple(vmem for _ in outputs),
            out_shape=tuple(outputs),
            scratch_shapes=list(scratch),
            cost_estimate=pl.CostEstimate(flops=flops, bytes_accessed=2 * bytes_moved, transcendentals=0),
            compiler_params=pltpu.CompilerParams(vmem_limit_bytes=VMEM_LIMIT),
            name=name,
        )(*[x[0] if isinstance(x, tuple) else x for x in inputs])

    def shaped(*shape, dtype=F32):
        return jax.ShapeDtypeStruct(shape, dtype)

    data = data_halves.reshape(2, views, rows, lateral)
    data, to_pair, to_other = pl.pallas_call(
        edge_kernel(views, rows, edge),
        in_specs=[pl.BlockSpec(memory_space=pltpu.HBM)],
        out_specs=(vmem, vmem, vmem),
        out_shape=(
            shaped(2, views, rows, lateral, dtype=BF),
            shaped(2, edge, lateral, dtype=BF),
            shaped(2, edge, lateral, dtype=BF),
        ),
        scratch_shapes=[pltpu.SemaphoreType.DMA((2 * views,))],
        compiler_params=pltpu.CompilerParams(vmem_limit_bytes=VMEM_LIMIT),
        name="edges",
    )(data)
    pair0, other0 = exchange(to_pair, to_other)

    kernels = psf_taps / jnp.sum(psf_taps, axis=-1, keepdims=True)
    band = shaped(views, 256, 256, dtype=BF)
    *mats, shape, one0, one1 = call(
        prep_kernel(views, taps, slab, depth, lateral),
        [(kernels.reshape(-1),)],
        [
            shaped(views * rows, ext_rows, dtype=BF),
            shaped(ext_rows, views * rows, dtype=BF),
            band,
            band,
            shaped(2, views * rows, 128),
            shaped(2, views, depth, 128),
            shaped(views, 2, 8, lateral),
            shaped(depth, 128),
            shaped(ext_rows, lateral),
            shaped(rows, lateral),
        ],
        "prep",
        flops=4 * 10**9,
    )

    (cycles,) = call(
        cycle_kernel(depth, half),
        [cycle_map],
        [shaped((depth // 2 + 1) * half, CYCLES, dtype=BF)],
        "cycles",
        flops=10**9,
    )

    held = [pltpu.VMEM((views * rows, lateral), BF)]
    firsts = []
    for h in range(2):
        own, to_pair, to_other = call(
            first_kernel(h, views, slab, rows, edge),
            [data, pair0, other0] + mats,
            [shaped(1, rows, lateral)] + [shaped(1, 2 * edge, lateral, dtype=BF)] * 2,
            f"first{h}",
            held,
            flops=4 * 10**9,
        )
        firsts.append((own, to_pair, to_other) + exchange(to_pair, to_other))

    angle = 2.0 * np.pi / lateral * np.arange(256)
    quarter = jnp.asarray(np.cos(angle).astype(np.float32).reshape(2, 128))
    grid_z = np.arange(depth)[:, None] * np.arange(depth)[None, :] % depth * (2.0 * np.pi / depth)
    wave = np.stack([np.cos(grid_z), np.sin(grid_z)]).astype(np.float32)
    wave = jnp.asarray(np.tile(wave, (1, 1, 128 // depth)))
    table = shaped(2 * rows, rows, dtype=BF)
    waves, back, table_hi, table_lo = call(
        table_kernel(slab, depth, lateral),
        [quarter, wave, firsts[1][0]],
        [shaped(lateral, lateral, dtype=BF), shaped(lateral, lateral, dtype=BF), table, table],
        "tables",
        flops=2 * 10**9,
    )

    seconds = []
    for h in range(2):
        own, to_pair, to_other, pair, other = firsts[h]
        est, part, to_pair, to_other = call(
            second_kernel(h, views, slab, rows, edge, lateral),
            [data, pair0, other0]
            + [own, to_pair, to_other, pair, other, shape, one0]
            + mats,
            [shaped(1, rows, lateral)] * 2 + [shaped(1, edge, lateral, dtype=BF)] * 2,
            f"second{h}",
            held,
            flops=4 * 10**9,
        )
        seconds.append((est, part) + exchange(to_pair, to_other))

    plane, top = shaped(rows, half), shaped(rows, 128)
    tables = [one1, waves, table_hi, table_lo]
    spectra = call(
        spectrum_kernel(views, slab, depth, lateral),
        [*seconds[0]] + tables,
        [plane, plane, top, top],
        "spectrum0",
        flops=10**9,
    )
    *mixed, sums = call(
        power_kernel(views, slab, depth, lateral, count),
        [*seconds[1]] + tables + [cycles, *spectra],
        [plane, plane, top, top, shaped(count, 3, CYCLES)],
        "spectrum1",
        flops=2 * 10**9,
    )
    sums = lax.all_to_all(sums, "tile", 0, 0)
    (joined,) = call(
        inverse_kernel(slab, depth, lateral, count),
        [(cutoff,), sums, cycle_map, *mixed, back, table_hi, table_lo],
        [shaped(rows, lateral)],
        "inverse",
        flops=10**9,
    )
    return joined.reshape(slab, depth, lateral)


def solution(mesh):
    in_specs = (
        P(None, None, ("groups", "tile"), None, None),
        P(),
        P(("groups", "tile"), None, None),
        P("groups"),
    )
    out_specs = P(("groups", "tile"), None, None)
    return jax.shard_map(body, mesh=mesh, in_specs=in_specs, out_specs=out_specs, check_vma=False)
```

```python
import jax
import jax.numpy as jnp
import numpy as np
from jax import lax
from jax.experimental import pallas as pl
from jax.experimental.pallas import tpu as pltpu
from jax.sharding import PartitionSpec as P


CYCLES = 256
BF = jnp.bfloat16
F32 = jnp.float32
VMEM_LIMIT = 32 * 1024 * 1024


def dot(a, b):
    return lax.dot_general(a, b, (((1,), (0,)), ((), ())), preferred_element_type=F32)


def iota(shape, dim):
    return lax.broadcasted_iota(jnp.int32, shape, dim)


def lookup(index, values):
    total = jnp.zeros(index.shape, F32)
    for place, value in values:
        total = jnp.where(index == place, value, total)
    return total


def shift_rows(x, by):
    count = x.shape[0]
    if by == 0:
        return x
    pad = jnp.zeros((abs(by), x.shape[1]), x.dtype)
    if by > 0:
        return jnp.concatenate([x[by:], pad], axis=0)
    return jnp.concatenate([pad, x[: count + by]], axis=0)


def prep_kernel(views, taps, slab, depth, lateral):
    radius = taps // 2
    group = 128 // depth
    ext = slab + 2 * radius
    rows = slab * depth
    scale = 1.0 / views

    def kernel(kern, a_ref, b_ref, t_ref, tt_ref, base_ref, off_ref, row_ref, w_ref, one0_ref, one1_ref):
        first = lax.axis_index("tile") * slab
        rows_total = lax.axis_size("tile") * slab

        all_taps = kern[...]

        def tap(v, axis, t):
            return all_taps[v * 3 + axis : v * 3 + axis + 1, t : t + 1]

        def spread(x):
            return jnp.concatenate([x] * (depth // 8), axis=0)

        def ones(v, axis, index, count, flip):
            summed = jnp.zeros(index.shape, F32)
            for t in range(taps):
                source = index + t - radius
                ok = (source >= 0) & (source < count)
                summed = summed + jnp.where(ok, tap(v, axis, taps - 1 - t if flip else t), 0.0)
            return summed

        row = iota((depth, 128), 0)
        lane = iota((depth, 128), 1)
        cell = lax.rem(lane, depth)
        slot8 = iota((8, 128), 1) // depth
        gap_z = cell - row + radius
        gap_zt = row - cell + radius
        lane8 = iota((8, 128), 1)
        gap8 = iota((8, 128), 0) - lane8
        zero = jnp.zeros((depth, 128), BF)
        tail = jnp.zeros((120, 128), F32)
        gains = []
        for v in range(views):
            band_z = lookup(gap_z, [(t, tap(v, 1, t)) for t in range(taps)])
            band_zt = lookup(gap_zt, [(t, tap(v, 1, t)) for t in range(taps)])

            def lane_taps(shift, sign, v=v):
                pairs = [(j, shift + sign * j) for j in range(group)]
                pairs = [(j, tap(v, 0, t)) for j, t in pairs if 0 <= t < taps]
                return lookup(slot8, pairs) if pairs else None

            blocks = {}
            for i in range(slab // 2):
                for g in range(ext // 2 // group + 1):
                    d = group * g - i
                    if d not in blocks:
                        weight = lane_taps(d, 1)
                        blocks[d] = zero if weight is None else (spread(weight) * band_z).astype(BF)
                    a_ref[pl.ds((v * slab // 2 + i) * depth, depth), pl.ds(g * 128, 128)] = blocks[d]
            for e in range(slab // 2 + 2 * radius):
                block = (spread(lane_taps(e, -1)) * band_zt).astype(BF)
                b_ref[pl.ds(e * depth, depth), pl.ds(v * 128, 128)] = block

            for flip, band_ref in ((False, t_ref), (True, tt_ref)):
                pairs = [(t, tap(v, 2, taps - 1 - t if flip else t)) for t in range(taps)]
                strip = lookup((gap8 + radius) & 127, pairs)
                strips = [strip] + [pltpu.roll(strip, 8 * n, 1) for n in range(1, 16)]
                first_strip = jnp.where(lane8 < 64, strips[0], 0.0)
                last_strip = jnp.where(lane8 >= 64, strips[15], 0.0)
                middle = jnp.concatenate([first_strip] + strips[1:15] + [last_strip], axis=0).astype(BF)
                upper = jnp.concatenate([tail, strips[15] - last_strip], axis=0).astype(BF)
                lower = jnp.concatenate([strips[0] - first_strip, tail], axis=0).astype(BF)
                for at, block in ((0, middle), (1, upper), (2, lower), (3, middle)):
                    at_rows, at_cols = pl.ds(at // 2 * 128, 128), pl.ds(at % 2 * 128, 128)
                    band_ref[v, at_rows, at_cols] = block

            mid = depth // 2
            sum_xz = jnp.sum(
                a_ref[pl.ds(v * rows // 2, depth), :].astype(F32)[mid : mid + 1], axis=1, keepdims=True
            )
            sum_y = jnp.sum(t_ref[v, 0:128, :].astype(F32)[64:65], axis=1, keepdims=True)
            gains.append(1.0 / (sum_xz * sum_y))

        def blur_z(v, x, flip):
            total = None
            for t in range(taps):
                term = shift_rows(x, t - radius) * tap(v, 1, taps - 1 - t if flip else t)
                total = term if total is None else total + term
            return total

        field0 = [ones(v, 1, row, depth, False) for v in range(views)]
        back0 = [blur_z(v, 1.0 / field0[v], True) for v in range(views)]
        shape = back0[0]
        for v in range(1, views):
            shape = shape + back0[v]
        shape = shape * scale
        w_ref[...] = shape
        field1 = [blur_z(v, shape, False) for v in range(views)]
        back1 = [blur_z(v, 1.0 / field1[v], True) for v in range(views)]

        x_out = iota((slab, 128), 0) + first
        x_ext = iota((ext, 128), 0) + (first - radius)
        y_row = iota((8, lateral), 1)
        edges = []
        for v in range(views):
            part_x = ones(v, 0, x_out, rows_total, False)
            for n, field in enumerate((field0, field1)):
                for i in range(slab):
                    at = pl.ds((v * slab + i) * depth, depth)
                    base_ref[n, at, :] = field[v] * part_x[i : i + 1]
                off_ref[n, v] = gains[v] / field[v]
            row_ref[v, 0] = ones(v, 2, y_row, lateral, False)
            row_ref[v, 1] = jnp.broadcast_to(gains[v], (8, lateral))
            edges.append((ones(v, 0, x_ext, rows_total, True) * scale, ones(v, 2, y_row, lateral, True)))
        for back, one_ref, low, high in ((back0, one0_ref, 0, ext), (back1, one1_ref, radius, radius + slab)):
            for e in range(low, high):
                terms = [back[v] * edges[v][0][e : e + 1] for v in range(views)]
                for j in range(lateral // 128):
                    total = None
                    for v in range(views):
                        term = terms[v]
                        if j in (0, lateral // 128 - 1):
                            term = term * edges[v][1][0:1, j * 128 : (j + 1) * 128]
                        total = term if total is None else total + term
                    one_ref[pl.ds((e - low) * depth, depth), pl.ds(j * 128, 128)] = total

    return kernel


def y_blur(x, band):
    rows = x.shape[0]
    stacked = jnp.concatenate([x[:, 0:256], x[:, 128:384], x[:, 256:512]], axis=0)
    wide = dot(stacked, band)
    left, mid, right = wide[:rows], wide[rows : 2 * rows], wide[2 * rows :]
    low = iota((rows, 128), 1) < 64
    return jnp.concatenate(
        [
            left[:, :128],
            jnp.where(low, left[:, 128:], mid[:, :128]),
            jnp.where(low, mid[:, 128:], right[:, :128]),
            right[:, 128:],
        ],
        axis=1,
    )


def level_of(x):
    total = jnp.sum(jnp.sum(x, axis=0, keepdims=True), axis=1, keepdims=True)
    return (total * (1.0 / x.size)).astype(BF).astype(F32)


def across(x, lateral):
    return jnp.concatenate([x] * (lateral // 128), axis=1)


def blur_back(n, h, views, slab, rows, level, data_ref, ext, mats, held):
    a_ref, b_ref, t_ref, tt_ref, base_ref, off_ref, row_ref = mats
    lateral = ext.shape[1]
    half = rows // 2
    seen = a_ref.shape[1]
    held[0] = dot(a_ref[...], ext[:seen]).astype(BF)
    held[1] = dot(a_ref[...], ext[half:]).astype(BF)
    for v in range(views):
        at = pl.ds(v * half, half)
        part = jnp.concatenate([held[0, at, :], held[1, at, :]], axis=0)
        base = across(base_ref[n, pl.ds(v * rows, rows), :], lateral) * (row_ref[v, 0, 0:1, :] * level)
        predicted = y_blur(part, t_ref[v]) + base
        scaled = data_ref[h, v].astype(F32) * row_ref[v, 1, 0:1, :]
        offset = across(jnp.concatenate([off_ref[n, v]] * slab, axis=0), lateral)
        quotient = (scaled / predicted - offset).astype(BF)
        back = y_blur(quotient, tt_ref[v]).astype(BF)
        held[0, at, :] = back[:half]
        held[1, at, :] = back[half:]
    low = dot(b_ref[...], held[0])
    high = dot(b_ref[...], held[1])
    return jnp.concatenate([low[:half], low[half:] + high[: seen - half], high[seen - half :]], axis=0)


def pick(even, from_pair, from_other, h=0):
    pair = from_pair[h].astype(F32)
    other = from_other[0].astype(F32)
    return jnp.where(even, other, pair), jnp.where(even, pair, other)


def put(even, low, high, to_pair, to_other, h=0, g=0):
    @pl.when(even)
    def _():
        to_pair[h] = high
        to_other[g] = low

    @pl.when(jnp.logical_not(even))
    def _():
        to_pair[h] = low
        to_other[g] = high


def is_even():
    return (lax.axis_index("tile") & 1) == 0


def has_sides():
    index = lax.axis_index("tile")
    return jnp.where(index > 0, 1.0, 0.0), jnp.where(index + 1 < lax.axis_size("tile"), 1.0, 0.0)


def mean_views(h, data_ref, views):
    total = data_ref[h, 0].astype(F32)
    for v in range(1, views):
        total = total + data_ref[h, v].astype(F32)
    return total * (1.0 / views)


def edge_kernel(views, rows, edge):
    def kernel(data_ref, *outs):
        even = is_even()
        to_pair = outs[-1]
        for h in range(2):
            est_ref, ext_ref, level_ref, to_other = outs[4 * h : 4 * h + 4]
            est = mean_views(h, data_ref, views)
            est_ref[...] = est
            put(even, est[:edge].astype(BF), est[rows - edge :].astype(BF), to_pair, to_other, h, 0)
            level = level_of(est)
            ext_ref[...] = (est - level).astype(BF)
            level_ref[...] = jnp.broadcast_to(level, level_ref.shape)

    return kernel


def first_kernel(h, views, slab, rows, edge):
    def kernel(data_ref, own_ext, level_ref, pair_ref, other_ref, *refs):
        mats, (own_ref, to_pair, to_other, held) = refs[:7], refs[7:]
        even = is_even()
        lo, hi = pick(even, pair_ref, other_ref, h)
        has_lo, has_hi = has_sides()
        level = level_ref[0:1, 0:1]
        lo = (lo - level * has_lo).astype(BF)
        hi = (hi - level * has_hi).astype(BF)
        ext = jnp.concatenate([lo, own_ext[...], hi], axis=0)
        part = blur_back(0, h, views, slab, rows, level, data_ref, ext, mats, held)
        own_ref[...] = part[edge : edge + rows]
        put(even, part[0 : 2 * edge].astype(BF), part[rows:].astype(BF), to_pair, to_other)

    return kernel


def second_kernel(h, views, slab, rows, edge, lateral):
    scale = 1.0 / views

    def kernel(
        data_ref, start_ref, level_ref, pair0_ref, other0_ref, own_ref, sent_pair, sent_other, pair_ref, other_ref, w_ref, one_ref, *refs
    ):
        mats, (est_ref, part_ref, to_pair, to_other, held) = refs[:7], refs[7:]
        even = is_even()
        has_lo, has_hi = has_sides()
        lo, hi = pick(even, pair0_ref, other0_ref, h)
        got_lo, got_hi = pick(even, pair_ref, other_ref)
        sent_lo, sent_hi = pick(even, sent_pair, sent_other)
        lo = lo * (one_ref[0:edge] + scale * (sent_lo[0:edge] + got_lo[0:edge]))
        hi = hi * (one_ref[edge + rows :] + scale * (sent_hi[edge:] + got_hi[edge:]))
        got = jnp.concatenate([got_lo[edge:], got_hi[0:edge]], axis=0)
        level = level_ref[0:1, 0:1]
        estimate = start_ref[...] * (one_ref[pl.ds(edge, rows)] + scale * (own_ref[...] + got))
        est_ref[...] = estimate
        shape = across(w_ref[...], lateral) * level
        shapes = jnp.concatenate([shape] * (edge // shape.shape[0]), axis=0)
        ext = jnp.concatenate(
            [
                lo - shapes * has_lo,
                estimate - jnp.concatenate([shape] * slab, axis=0),
                hi - shapes * has_hi,
            ],
            axis=0,
        )
        part = blur_back(1, h, views, slab, rows, level, data_ref, ext.astype(BF), mats, held)
        part_ref[...] = part[edge : edge + rows]
        put(even, part[0:edge].astype(BF), part[edge + rows :].astype(BF), to_pair, to_other)

    return kernel


def table_kernel(slab, depth, lateral):
    half = lateral // 2

    def kernel(quarter_ref, wave_ref, _, waves_ref, back_ref, high_ref, low_ref):
        steps = [jnp.broadcast_to(quarter_ref[0:1, :], (8, 128)), jnp.broadcast_to(quarter_ref[1:2, :], (8, 128))]
        row8 = iota((8, 128), 0)
        odd_row = (iota((16, 128), 0) & 1) == 1
        odd_lane = (iota((16, 128), 1) & 1) == 1
        for j in range(half // 128):
            lane = iota((8, 128), 1) + j * 128
            phase = (row8 * lane) & (lateral - 1)
            for i in range(half // 16):
                pair = []
                for _ in range(2):
                    near, turn = phase & 127, phase // 128
                    g0 = jnp.take_along_axis(steps[0], near, axis=1)
                    g1 = jnp.take_along_axis(steps[1], near, axis=1)
                    odd = (turn & 1) == 1
                    cos = jnp.where(odd, g1, g0)
                    sin = jnp.where(odd, g0, g1)
                    pair.append((jnp.where(turn >= 2, -cos, cos), jnp.where((turn == 0) | (turn == 3), -sin, sin)))
                    phase = (phase + lane * 8) & (lateral - 1)
                cos = jnp.concatenate([pair[0][0], pair[1][0]], axis=0)
                sin = jnp.concatenate([pair[0][1], pair[1][1]], axis=0)
                ahead, behind = sin, -sin
                if j == 0:
                    ahead = jnp.where(iota((16, 128), 1) == 0, jnp.where(odd_row, -1.0, 1.0), sin)
                if i == 0:
                    behind = jnp.where(iota((16, 128), 0) == 0, jnp.where(odd_lane, -1.0, 1.0), behind)
                here, there = pl.ds(i * 16, 16), pl.ds(half + i * 16, 16)
                left, right = pl.ds(j * 128, 128), pl.ds(half + j * 128, 128)
                waves_ref[here, left] = cos.astype(BF)
                waves_ref[here, right] = ahead.astype(BF)
                waves_ref[there, left] = jnp.where(odd_lane, -cos, cos).astype(BF)
                waves_ref[there, right] = jnp.where(odd_lane, -ahead, ahead).astype(BF)
                back_ref[here, left] = cos.astype(BF)
                back_ref[here, right] = jnp.where(odd_row, -cos, cos).astype(BF)
                back_ref[there, left] = behind.astype(BF)
                back_ref[there, right] = jnp.where(odd_row, -behind, behind).astype(BF)
        slot = iota((depth, 128), 1) // depth
        group = 128 // depth
        for kind in range(2):
            wave = wave_ref[kind]
            high = wave.astype(BF).astype(F32)
            for i in range(slab):
                for g in range(slab * depth // 128):
                    at = (pl.ds((kind * slab + i) * depth, depth), pl.ds(g * 128, 128))
                    here = slot == i - group * g
                    high_ref[at] = jnp.where(here, high, 0.0).astype(BF)
                    low_ref[at] = jnp.where(here, wave - high, 0.0).astype(BF)

    return kernel


def split_dot(table_hi, table_lo, x):
    x_hi = x.astype(BF)
    x_lo = (x - x_hi.astype(F32)).astype(BF)
    return dot(table_hi, x_hi) + dot(table_hi, x_lo) + dot(table_lo, x_hi)


def spectrum(even, scale, rows, half, est_ref, part_ref, pair_ref, other_ref, one_ref, waves_ref, high_ref, low_ref):
    got_lo, got_hi = pick(even, pair_ref, other_ref)
    got = jnp.concatenate([got_lo, got_hi], axis=0)
    estimate = est_ref[...] * (one_ref[...] + scale * (part_ref[...] + got))
    row = dot(estimate.astype(BF), waves_ref[...])
    from_cos = split_dot(high_ref[...], low_ref[...], row[:, :half])
    from_sin = split_dot(high_ref[...], low_ref[...], row[:, half:])
    first = iota((rows, half), 1) == 0
    sin_cos = from_sin[:rows]
    sin_sin = from_sin[rows:]
    real = from_cos[:rows] - jnp.where(first, 0.0, sin_sin)
    imag = -from_cos[rows:] - jnp.where(first, 0.0, sin_cos)
    top = iota((rows, 128), 1) == 0
    top_real = jnp.where(top, sin_cos[:, :128], 0.0)
    top_imag = jnp.where(top, -sin_sin[:, :128], 0.0)
    return real, imag, top_real, top_imag


def spectrum_kernel(views, slab, depth, lateral):
    rows, half = slab * depth, lateral // 2

    def kernel(est_ref, part_ref, pair_ref, other_ref, one_ref, waves_ref, high_ref, low_ref, *outs):
        even = is_even()
        args = (est_ref, part_ref, pair_ref, other_ref, one_ref, waves_ref, high_ref, low_ref)
        for ref, value in zip(outs, spectrum(even, 1.0 / views, rows, half, *args)):
            ref[...] = value

    return kernel


def cycle_kernel(depth, half):
    def kernel(map_ref, _, cycle_ref):
        columns = jnp.transpose(map_ref[0, :, 0:half].astype(F32))
        cycle = iota((128, CYCLES), 1).astype(F32)
        zero = jnp.zeros((128, 128), BF)
        for k in range(depth // 2 + 1):
            low = columns[:128, k : k + 1] == cycle
            high = columns[128:, k : k + 1] == cycle[:, 128:]
            cycle_ref[pl.ds(k * half, 128), :] = jnp.where(low, 1.0, 0.0).astype(BF)
            cycle_ref[pl.ds(k * half + 128, 128), 0:128] = zero
            cycle_ref[pl.ds(k * half + 128, 128), 128:256] = jnp.where(high, 1.0, 0.0).astype(BF)

    return kernel


def power_kernel(views, slab, depth, lateral, count):
    rows, half = slab * depth, lateral // 2

    def kernel(
        est_ref,
        part_ref,
        pair_ref,
        other_ref,
        one_ref,
        waves_ref,
        high_ref,
        low_ref,
        cycle_ref,
        re_ref,
        im_ref,
        tre_ref,
        tim_ref,
        mre_ref,
        mim_ref,
        mtre_ref,
        mtim_ref,
        sum_ref,
    ):
        even = is_even()
        args = (est_ref, part_ref, pair_ref, other_ref, one_ref, waves_ref, high_ref, low_ref)
        re1, im1, tre1, tim1 = spectrum(even, 1.0 / views, rows, half, *args)
        re0, im0, tre0, tim0 = re_ref[...], im_ref[...], tre_ref[...], tim_ref[...]
        mre_ref[...] = 0.5 * (re0 + re1)
        mim_ref[...] = 0.5 * (im0 + im1)
        mtre_ref[...] = 0.5 * (tre0 + tre1)
        mtim_ref[...] = 0.5 * (tim0 + tim1)

        def over_slab(x):
            total = x[0:depth]
            for s in range(1, slab):
                total = total + x[s * depth : (s + 1) * depth]
            return total

        twice = jnp.where(iota((depth, half), 1) == 0, 1.0, 2.0)
        powers, tops = [], []
        for a, b, c, d in (
            (re0, re1, im0, im1),
            (re0, re0, im0, im0),
            (re1, re1, im1, im1),
        ):
            powers.append(over_slab(a * b + c * d) * twice)
        for a, b, c, d in (
            (tre0, tre1, tim0, tim1),
            (tre0, tre0, tim0, tim0),
            (tre1, tre1, tim1, tim1),
        ):
            tops.append(jnp.sum(over_slab(a * b + c * d), axis=0, keepdims=True))
        top = jnp.sum(jnp.concatenate(tops, axis=0), axis=1, keepdims=True)
        terms = []
        for k in range(depth // 2 + 1):
            other = depth - k
            fold = [p[k : k + 1] + p[other : other + 1] if 0 < k < other else p[k : k + 1] for p in powers]
            terms.append(jnp.concatenate(fold, axis=0))
        term = jnp.concatenate(terms, axis=1)
        high = term.astype(BF).astype(F32)
        middle = (term - high).astype(BF).astype(F32)
        low = term - high - middle
        total = dot(jnp.concatenate([high, middle, low], axis=0).astype(BF), cycle_ref[...])
        last = jnp.where(iota((3, CYCLES), 1) == CYCLES - 1, top, 0.0)
        total = total[0:3] + total[3:6] + total[6:9] + last
        for i in range(count):
            sum_ref[i] = total

    return kernel


def inverse_kernel(slab, depth, lateral, count):
    rows, half = slab * depth, lateral // 2

    def kernel(cut_ref, sum_ref, map_ref, mre_ref, mim_ref, mtre_ref, mtim_ref, back_ref, high_ref, low_ref, out_ref):
        total = sum_ref[0]
        for i in range(1, count):
            total = total + sum_ref[i]
        cross, power0, power1 = total[0:1], total[1:2], total[2:3]
        corr = cross / (jnp.sqrt(power0) * jnp.sqrt(power1))
        weight = jnp.where(iota((1, CYCLES), 1) <= cut_ref[0], corr, 0.0)
        low = jnp.broadcast_to(weight[:, 0:128], (depth, 128))
        high = jnp.broadcast_to(weight[:, 128:256], (depth, 128))
        pieces = []
        for j in range(half // 128):
            cell = map_ref[0, :, pl.ds(j * 128, 128)]
            near = cell & 127
            found = jnp.where(
                cell < 128,
                jnp.take_along_axis(low, near, axis=1),
                jnp.take_along_axis(high, near, axis=1),
            )
            twice = jnp.where(iota((depth, 128), 1) + j * 128 == 0, 1.0, 2.0)
            pieces.append(found * twice)
        cells = jnp.concatenate(pieces, axis=1)
        cells = jnp.concatenate([cells] * slab, axis=0)
        last = weight[:, CYCLES - 1 : CYCLES]
        re = mre_ref[...] * cells
        im = mim_ref[...] * cells
        re = jnp.concatenate([re[:, :128] - mtim_ref[...] * last, re[:, 128:]], axis=1)
        im = jnp.concatenate([im[:, :128] + mtre_ref[...] * last, im[:, 128:]], axis=1)
        from_re = split_dot(high_ref[...], low_ref[...], re)
        from_im = split_dot(high_ref[...], low_ref[...], im)
        inner_re = (from_re[:rows] - from_im[rows:]).astype(BF)
        inner_im = (from_re[rows:] + from_im[:rows]).astype(BF)
        joined = dot(inner_re, back_ref[0:half]) + dot(inner_im, back_ref[half:lateral])
        out_ref[...] = joined * (1.0 / (depth * lateral))

    return kernel


def body(data_halves, psf_taps, cycle_map, cutoff):
    _, views, slab, depth, lateral = data_halves.shape
    taps = psf_taps.shape[-1]
    radius = taps // 2
    rows, edge = slab * depth, radius * depth
    ext_rows = rows + 2 * edge
    half = lateral // 2
    count = lax.axis_size("tile")
    pairs = [(i, i ^ 1) for i in range(count)]
    others = [(i, i + 1) for i in range(1, count - 1, 2)]
    others = others + [(b, a) for a, b in others]

    def to_other(array):
        return lax.ppermute(array, "tile", others)

    def to_pair(array):
        return lax.ppermute(array, "tile", pairs)

    def exchange(for_pair, for_other):
        other = to_other(for_other)
        return to_pair(for_pair), other

    vmem = pl.BlockSpec(memory_space=pltpu.VMEM)
    scalars = pl.BlockSpec(memory_space=pltpu.SMEM)

    def call(kernel, inputs, outputs, scratch=(), flops=0):
        bytes_moved = sum(int(np.prod(s.shape)) * s.dtype.itemsize for s in outputs)
        return pl.pallas_call(
            kernel,
            in_specs=[scalars if isinstance(x, tuple) else vmem for x in inputs],
            out_specs=tuple(vmem for _ in outputs),
            out_shape=tuple(outputs),
            scratch_shapes=list(scratch),
            cost_estimate=pl.CostEstimate(flops=flops, bytes_accessed=2 * bytes_moved, transcendentals=0),
            compiler_params=pltpu.CompilerParams(vmem_limit_bytes=VMEM_LIMIT),
        )(*[x[0] if isinstance(x, tuple) else x for x in inputs])

    def shaped(*shape, dtype=F32):
        return jax.ShapeDtypeStruct(shape, dtype)

    data = data_halves.reshape(2, views, rows, lateral)
    side = shaped(1, edge, lateral, dtype=BF)
    plane = shaped(rows, lateral)
    begun = call(
        edge_kernel(views, rows, edge),
        [data],
        [plane, shaped(rows, lateral, dtype=BF), shaped(8, 128), side] * 2
        + [shaped(2, edge, lateral, dtype=BF)],
        flops=10**9,
    )
    means, own_exts, levels = begun[0:8:4], begun[1:8:4], begun[2:8:4]
    others0 = [to_other(begun[3]), to_other(begun[7])]
    pair0 = to_pair(begun[8])
    starts = [(pair0, other) for other in others0]

    kernels = psf_taps / jnp.sum(psf_taps, axis=-1, keepdims=True)
    band = shaped(views, 256, 256, dtype=BF)
    *mats, shape, one0, one1 = call(
        prep_kernel(views, taps, slab, depth, lateral),
        [kernels.reshape(3 * views, taps)],
        [
            shaped(views * rows // 2, rows // 2 + 2 * edge, dtype=BF),
            shaped(rows // 2 + 2 * edge, views * rows // 2, dtype=BF),
            band,
            band,
            shaped(2, views * rows, 128),
            shaped(2, views, depth, 128),
            shaped(views, 2, 8, lateral),
            shaped(depth, 128),
            shaped(ext_rows, lateral),
            shaped(rows, lateral),
        ],
        flops=4 * 10**9,
    )

    held = [pltpu.VMEM((2, views * rows // 2, lateral), BF)]
    firsts = []
    for h in range(2):
        own, for_pair, for_other = call(
            first_kernel(h, views, slab, rows, edge),
            [data, own_exts[h], levels[h], *starts[h]] + mats,
            [shaped(rows, lateral)] + [shaped(1, 2 * edge, lateral, dtype=BF)] * 2,
            held,
            flops=4 * 10**9,
        )
        firsts.append((own, for_pair, for_other) + exchange(for_pair, for_other))

    angle = 2.0 * np.pi / lateral * np.arange(256)
    quarter = jnp.asarray(np.cos(angle).astype(np.float32).reshape(2, 128))
    grid_z = np.arange(depth)[:, None] * np.arange(depth)[None, :] % depth * (2.0 * np.pi / depth)
    wave = np.stack([np.cos(grid_z), np.sin(grid_z)]).astype(np.float32)
    wave = jnp.asarray(np.tile(wave, (1, 1, 128 // depth)))
    table = shaped(2 * rows, rows, dtype=BF)
    seconds = []
    for h in range(2):
        est, part, for_pair, for_other = call(
            second_kernel(h, views, slab, rows, edge, lateral),
            [data, means[h], levels[h], *starts[h]]
            + [*firsts[h], shape, one0]
            + mats,
            [shaped(rows, lateral)] * 2 + [shaped(1, edge, lateral, dtype=BF)] * 2,
            held,
            flops=4 * 10**9,
        )
        seconds.append((est, part) + exchange(for_pair, for_other))

    waves, back, table_hi, table_lo = call(
        table_kernel(slab, depth, lateral),
        [quarter, wave, seconds[1][0]],
        [shaped(lateral, lateral, dtype=BF), shaped(lateral, lateral, dtype=BF), table, table],
        flops=2 * 10**9,
    )

    (cycles,) = call(
        cycle_kernel(depth, half),
        [cycle_map, seconds[1][0]],
        [shaped((depth // 2 + 1) * half, CYCLES, dtype=BF)],
        flops=10**9,
    )

    plane, top = shaped(rows, half), shaped(rows, 128)
    tables = [one1, waves, table_hi, table_lo]
    spectra = call(
        spectrum_kernel(views, slab, depth, lateral), [*seconds[0]] + tables, [plane, plane, top, top], flops=10**9
    )
    *mixed, sums = call(
        power_kernel(views, slab, depth, lateral, count),
        [*seconds[1]] + tables + [cycles, *spectra],
        [plane, plane, top, top, shaped(count, 3, CYCLES)],
        flops=2 * 10**9,
    )
    sums = lax.all_to_all(sums, "tile", 0, 0)
    (joined,) = call(
        inverse_kernel(slab, depth, lateral, count),
        [(cutoff,), sums, cycle_map, *mixed, back, table_hi, table_lo],
        [shaped(rows, lateral)],
        flops=10**9,
    )
    return joined.reshape(slab, depth, lateral)


def solution(mesh):
    in_specs = (
        P(None, None, ("groups", "tile"), None, None),
        P(),
        P(("groups", "tile"), None, None),
        P("groups"),
    )
    out_specs = P(("groups", "tile"), None, None)

    return jax.shard_map(body, mesh=mesh, in_specs=in_specs, out_specs=out_specs, check_vma=False)
```

```python
import jax
import jax.numpy as jnp
import numpy as np
from jax import lax
from jax.experimental import pallas as pl
from jax.experimental.pallas import tpu as pltpu
from jax.sharding import PartitionSpec as P


CYCLES = 256
BF = jnp.bfloat16
F32 = jnp.float32
VMEM_LIMIT = 32 * 1024 * 1024


def dot(a, b):
    return lax.dot_general(a, b, (((1,), (0,)), ((), ())), preferred_element_type=F32)


def iota(shape, dim):
    return lax.broadcasted_iota(jnp.int32, shape, dim)


def lookup(index, values):
    total = jnp.zeros(index.shape, F32)
    for place, value in values:
        total = jnp.where(index == place, value, total)
    return total


def shift_rows(x, by):
    count = x.shape[0]
    if by == 0:
        return x
    pad = jnp.zeros((abs(by), x.shape[1]), x.dtype)
    if by > 0:
        return jnp.concatenate([x[by:], pad], axis=0)
    return jnp.concatenate([pad, x[: count + by]], axis=0)


def prep_kernel(views, taps, slab, depth, lateral):
    radius = taps // 2
    group = 128 // depth
    ext = slab + 2 * radius
    rows = slab * depth
    scale = 1.0 / views

    def kernel(kern, a_ref, b_ref, t_ref, tt_ref, base_ref, off_ref, row_ref, w_ref, one0_ref, one1_ref):
        first = lax.axis_index("tile") * slab
        rows_total = lax.axis_size("tile") * slab

        all_taps = [kern[axis] / jnp.sum(kern[axis], axis=1, keepdims=True) for axis in range(3)]

        def tap(v, axis, t):
            return all_taps[axis][v : v + 1, t : t + 1]

        def spread(x):
            return jnp.concatenate([x] * (depth // 8), axis=0)

        def ones(v, axis, index, count, flip):
            summed = jnp.zeros(index.shape, F32)
            for t in range(taps):
                source = index + t - radius
                ok = (source >= 0) & (source < count)
                summed = summed + jnp.where(ok, tap(v, axis, taps - 1 - t if flip else t), 0.0)
            return summed

        row = iota((depth, 128), 0)
        lane = iota((depth, 128), 1)
        cell = lax.rem(lane, depth)
        slot8 = iota((8, 128), 1) // depth
        gap_z = cell - row + radius
        gap_zt = row - cell + radius
        lane8 = iota((8, 128), 1)
        gap8 = iota((8, 128), 0) - lane8
        zero = jnp.zeros((depth, 128), BF)
        tail = jnp.zeros((120, 128), F32)
        gains = []
        for v in range(views):
            band_z = lookup(gap_z, [(t, tap(v, 1, t)) for t in range(taps)])
            band_zt = lookup(gap_zt, [(t, tap(v, 1, t)) for t in range(taps)])

            def lane_taps(shift, sign, v=v):
                pairs = [(j, shift + sign * j) for j in range(group)]
                pairs = [(j, tap(v, 0, t)) for j, t in pairs if 0 <= t < taps]
                return lookup(slot8, pairs) if pairs else None

            blocks = {}
            for i in range(slab // 2):
                for g in range(ext // 2 // group + 1):
                    d = group * g - i
                    if d not in blocks:
                        weight = lane_taps(d, 1)
                        blocks[d] = zero if weight is None else (spread(weight) * band_z).astype(BF)
                    a_ref[pl.ds((v * slab // 2 + i) * depth, depth), pl.ds(g * 128, 128)] = blocks[d]
            for e in range(slab // 2 + 2 * radius):
                block = (spread(lane_taps(e, -1)) * band_zt).astype(BF)
                b_ref[pl.ds(e * depth, depth), pl.ds(v * 128, 128)] = block

            for flip, band_ref in ((False, t_ref), (True, tt_ref)):
                pairs = [(t, tap(v, 2, taps - 1 - t if flip else t)) for t in range(taps)]
                strip = lookup((gap8 + radius) & 127, pairs)
                strips = [strip] + [pltpu.roll(strip, 8 * n, 1) for n in range(1, 16)]
                first_strip = jnp.where(lane8 < 64, strips[0], 0.0)
                last_strip = jnp.where(lane8 >= 64, strips[15], 0.0)
                middle = jnp.concatenate([first_strip] + strips[1:15] + [last_strip], axis=0).astype(BF)
                upper = jnp.concatenate([tail, strips[15] - last_strip], axis=0).astype(BF)
                lower = jnp.concatenate([strips[0] - first_strip, tail], axis=0).astype(BF)
                for at, block in ((0, middle), (1, upper), (2, lower), (3, middle)):
                    at_rows, at_cols = pl.ds(at // 2 * 128, 128), pl.ds(at % 2 * 128, 128)
                    band_ref[v, at_rows, at_cols] = block

            mid = depth // 2
            sum_xz = jnp.sum(
                a_ref[pl.ds(v * rows // 2, depth), :].astype(F32)[mid : mid + 1], axis=1, keepdims=True
            )
            sum_y = jnp.sum(t_ref[v, 0:128, :].astype(F32)[64:65], axis=1, keepdims=True)
            gains.append(1.0 / (sum_xz * sum_y))

        def blur_z(v, x, flip):
            total = None
            for t in range(taps):
                term = shift_rows(x, t - radius) * tap(v, 1, taps - 1 - t if flip else t)
                total = term if total is None else total + term
            return total

        field0 = [ones(v, 1, row, depth, False) for v in range(views)]
        back0 = [blur_z(v, 1.0 / field0[v], True) for v in range(views)]
        shape = back0[0]
        for v in range(1, views):
            shape = shape + back0[v]
        shape = shape * scale
        w_ref[...] = shape
        field1 = [blur_z(v, shape, False) for v in range(views)]
        back1 = [blur_z(v, 1.0 / field1[v], True) for v in range(views)]

        x_out = iota((slab, 128), 0) + first
        x_ext = iota((ext, 128), 0) + (first - radius)
        y_row = iota((8, lateral), 1)
        edges = []
        for v in range(views):
            part_x = ones(v, 0, x_out, rows_total, False)
            for n, field in enumerate((field0, field1)):
                for i in range(slab):
                    at = pl.ds((v * slab + i) * depth, depth)
                    base_ref[n, at, :] = field[v] * part_x[i : i + 1]
                off_ref[n, v] = gains[v] / field[v]
            row_ref[v, 0] = ones(v, 2, y_row, lateral, False)
            row_ref[v, 1] = jnp.broadcast_to(gains[v], (8, lateral))
            edges.append((ones(v, 0, x_ext, rows_total, True) * scale, ones(v, 2, y_row, lateral, True)))
        for back, one_ref, low, high in ((back0, one0_ref, 0, ext), (back1, one1_ref, radius, radius + slab)):
            for e in range(low, high):
                terms = [back[v] * edges[v][0][e : e + 1] for v in range(views)]
                for j in range(lateral // 128):
                    total = None
                    for v in range(views):
                        term = terms[v]
                        if j in (0, lateral // 128 - 1):
                            term = term * edges[v][1][0:1, j * 128 : (j + 1) * 128]
                        total = term if total is None else total + term
                    one_ref[pl.ds((e - low) * depth, depth), pl.ds(j * 128, 128)] = total

    return kernel


def y_blur(x, band):
    rows = x.shape[0]
    stacked = jnp.concatenate([x[:, 0:256], x[:, 128:384], x[:, 256:512]], axis=0)
    wide = dot(stacked, band)
    left, mid, right = wide[:rows], wide[rows : 2 * rows], wide[2 * rows :]
    low = iota((rows, 128), 1) < 64
    return jnp.concatenate(
        [
            left[:, :128],
            jnp.where(low, left[:, 128:], mid[:, :128]),
            jnp.where(low, mid[:, 128:], right[:, :128]),
            right[:, 128:],
        ],
        axis=1,
    )


def level_of(x):
    total = jnp.sum(jnp.sum(x, axis=0, keepdims=True), axis=1, keepdims=True)
    return (total * (1.0 / x.size)).astype(BF).astype(F32)


def across(x, lateral):
    return jnp.concatenate([x] * (lateral // 128), axis=1)


def blur_back(n, h, views, slab, rows, level, data_ref, ext, mats, held):
    a_ref, b_ref, t_ref, tt_ref, base_ref, off_ref, row_ref = mats
    lateral = ext.shape[1]
    half = rows // 2
    seen = a_ref.shape[1]
    held[0] = dot(a_ref[...], ext[:seen]).astype(BF)
    held[1] = dot(a_ref[...], ext[half:]).astype(BF)
    for v in range(views):
        at = pl.ds(v * half, half)
        part = jnp.concatenate([held[0, at, :], held[1, at, :]], axis=0)
        base = across(base_ref[n, pl.ds(v * rows, rows), :], lateral) * (row_ref[v, 0, 0:1, :] * level)
        predicted = y_blur(part, t_ref[v]) + base
        scaled = data_ref[h, v].astype(F32) * row_ref[v, 1, 0:1, :]
        offset = across(jnp.concatenate([off_ref[n, v]] * slab, axis=0), lateral)
        quotient = (scaled / predicted - offset).astype(BF)
        back = y_blur(quotient, tt_ref[v]).astype(BF)
        held[0, at, :] = back[:half]
        held[1, at, :] = back[half:]
    low = dot(b_ref[...], held[0])
    high = dot(b_ref[...], held[1])
    return jnp.concatenate([low[:half], low[half:] + high[: seen - half], high[seen - half :]], axis=0)


def pick(even, from_pair, from_other, h=0):
    pair = from_pair[h].astype(F32)
    other = from_other[0].astype(F32)
    return jnp.where(even, other, pair), jnp.where(even, pair, other)


def put(even, low, high, to_pair, to_other, h=0, g=0):
    to_pair[h] = jnp.where(even, high, low).astype(BF)
    to_other[g] = jnp.where(even, low, high).astype(BF)


def is_even():
    return (lax.axis_index("tile") & 1) == 0


def has_sides():
    index = lax.axis_index("tile")
    return jnp.where(index > 0, 1.0, 0.0), jnp.where(index + 1 < lax.axis_size("tile"), 1.0, 0.0)


def mean_views(h, data_ref, views):
    total = data_ref[h, 0].astype(F32)
    for v in range(1, views):
        total = total + data_ref[h, v].astype(F32)
    return total * (1.0 / views)


def edge_kernel(views, rows, edge):
    def kernel(data_ref, *outs):
        even = is_even()
        to_pair = outs[-1]
        for h in range(2):
            est_ref, ext_ref, level_ref, to_other = outs[4 * h : 4 * h + 4]
            est = mean_views(h, data_ref, views)
            est_ref[...] = est
            put(even, est[:edge], est[rows - edge :], to_pair, to_other, h, 0)
            level = level_of(est)
            ext_ref[...] = (est - level).astype(BF)
            level_ref[...] = jnp.broadcast_to(level, level_ref.shape)

    return kernel


def first_kernel(h, views, slab, rows, edge):
    def kernel(data_ref, own_ext, level_ref, pair_ref, other_ref, *refs):
        mats, (own_ref, to_pair, to_other, held) = refs[:7], refs[7:]
        even = is_even()
        lo, hi = pick(even, pair_ref, other_ref, h)
        has_lo, has_hi = has_sides()
        level = level_ref[0:1, 0:1]
        lo = (lo - level * has_lo).astype(BF)
        hi = (hi - level * has_hi).astype(BF)
        ext = jnp.concatenate([lo, own_ext[...], hi], axis=0)
        part = blur_back(0, h, views, slab, rows, level, data_ref, ext, mats, held)
        own_ref[...] = part[edge : edge + rows]
        put(even, part[0 : 2 * edge], part[rows:], to_pair, to_other)

    return kernel


def second_kernel(h, views, slab, rows, edge, lateral):
    scale = 1.0 / views

    def kernel(
        data_ref, start_ref, level_ref, pair0_ref, other0_ref, own_ref, sent_pair, sent_other, pair_ref, other_ref, w_ref, one_ref, *refs
    ):
        mats, (est_ref, part_ref, to_pair, to_other, held) = refs[:7], refs[7:]
        even = is_even()
        has_lo, has_hi = has_sides()
        lo, hi = pick(even, pair0_ref, other0_ref, h)
        got_lo, got_hi = pick(even, pair_ref, other_ref)
        sent_lo, sent_hi = pick(even, sent_pair, sent_other)
        lo = lo * (one_ref[0:edge] + scale * (sent_lo[0:edge] + got_lo[0:edge]))
        hi = hi * (one_ref[edge + rows :] + scale * (sent_hi[edge:] + got_hi[edge:]))
        got = jnp.concatenate([got_lo[edge:], got_hi[0:edge]], axis=0)
        level = level_ref[0:1, 0:1]
        estimate = start_ref[...] * (one_ref[pl.ds(edge, rows)] + scale * (own_ref[...] + got))
        est_ref[...] = estimate
        shape = across(w_ref[...], lateral) * level
        shapes = jnp.concatenate([shape] * (edge // shape.shape[0]), axis=0)
        ext = jnp.concatenate(
            [
                lo - shapes * has_lo,
                estimate - jnp.concatenate([shape] * slab, axis=0),
                hi - shapes * has_hi,
            ],
            axis=0,
        )
        part = blur_back(1, h, views, slab, rows, level, data_ref, ext.astype(BF), mats, held)
        part_ref[...] = part[edge : edge + rows]
        put(even, part[0:edge], part[edge + rows :], to_pair, to_other)

    return kernel


def table_kernel(depth, lateral):
    half = lateral // 2

    def kernel(quarter_ref, wave_ref, _, waves_ref, back_ref, high_ref, low_ref):
        steps = [jnp.broadcast_to(quarter_ref[0:1, :], (8, 128)), jnp.broadcast_to(quarter_ref[1:2, :], (8, 128))]
        row8 = iota((8, 128), 0)
        odd_row = (iota((16, 128), 0) & 1) == 1
        odd_lane = (iota((16, 128), 1) & 1) == 1
        for j in range(half // 128):
            lane = iota((8, 128), 1) + j * 128
            phase = (row8 * lane) & (lateral - 1)
            for i in range(half // 16):
                pair = []
                for _ in range(2):
                    near, turn = phase & 127, phase // 128
                    g0 = jnp.take_along_axis(steps[0], near, axis=1)
                    g1 = jnp.take_along_axis(steps[1], near, axis=1)
                    odd = (turn & 1) == 1
                    cos = jnp.where(odd, g1, g0)
                    sin = jnp.where(odd, g0, g1)
                    pair.append((jnp.where(turn >= 2, -cos, cos), jnp.where((turn == 0) | (turn == 3), -sin, sin)))
                    phase = (phase + lane * 8) & (lateral - 1)
                cos = jnp.concatenate([pair[0][0], pair[1][0]], axis=0)
                sin = jnp.concatenate([pair[0][1], pair[1][1]], axis=0)
                ahead, behind = sin, -sin
                if j == 0:
                    ahead = jnp.where(iota((16, 128), 1) == 0, jnp.where(odd_row, -1.0, 1.0), sin)
                if i == 0:
                    behind = jnp.where(iota((16, 128), 0) == 0, jnp.where(odd_lane, -1.0, 1.0), behind)
                here, there = pl.ds(i * 16, 16), pl.ds(half + i * 16, 16)
                left, right = pl.ds(j * 128, 128), pl.ds(half + j * 128, 128)
                waves_ref[here, left] = cos.astype(BF)
                waves_ref[here, right] = ahead.astype(BF)
                waves_ref[there, left] = jnp.where(odd_lane, -cos, cos).astype(BF)
                waves_ref[there, right] = jnp.where(odd_lane, -ahead, ahead).astype(BF)
                back_ref[here, left] = cos.astype(BF)
                back_ref[here, right] = jnp.where(odd_row, -cos, cos).astype(BF)
                back_ref[there, left] = behind.astype(BF)
                back_ref[there, right] = jnp.where(odd_row, -behind, behind).astype(BF)
        slot = iota((depth, 128), 1) // depth
        group = 128 // depth
        for kind in range(2):
            wave = wave_ref[kind]
            high = wave.astype(BF).astype(F32)
            for i in range(group):
                at = pl.ds((kind * group + i) * depth, depth)
                here = slot == i
                high_ref[at, :] = jnp.where(here, high, 0.0).astype(BF)
                low_ref[at, :] = jnp.where(here, wave - high, 0.0).astype(BF)

    return kernel


def z_waves(table_hi, table_lo, x):
    cosines, sines = [], []
    for at in range(0, x.shape[0], 128):
        part = x[at : at + 128]
        high = part.astype(BF)
        low = (part - high.astype(F32)).astype(BF)
        total = dot(table_hi, high) + dot(table_hi, low) + dot(table_lo, high)
        cosines.append(total[:128])
        sines.append(total[128:])
    return jnp.concatenate(cosines, axis=0), jnp.concatenate(sines, axis=0)


def spectrum(even, scale, rows, half, est_ref, part_ref, pair_ref, other_ref, one_ref, waves_ref, high_ref, low_ref):
    got_lo, got_hi = pick(even, pair_ref, other_ref)
    got = jnp.concatenate([got_lo, got_hi], axis=0)
    estimate = est_ref[...] * (one_ref[...] + scale * (part_ref[...] + got))
    row = dot(estimate.astype(BF), waves_ref[...])
    cos_cos, cos_sin = z_waves(high_ref[...], low_ref[...], row[:, :half])
    sin_cos, sin_sin = z_waves(high_ref[...], low_ref[...], row[:, half:])
    first = iota((rows, half), 1) == 0
    real = cos_cos - jnp.where(first, 0.0, sin_sin)
    imag = -cos_sin - jnp.where(first, 0.0, sin_cos)
    top = iota((rows, 128), 1) == 0
    top_real = jnp.where(top, sin_cos[:, :128], 0.0)
    top_imag = jnp.where(top, -sin_sin[:, :128], 0.0)
    return real, imag, top_real, top_imag


def spectrum_kernel(views, slab, depth, lateral):
    rows, half = slab * depth, lateral // 2

    def kernel(est_ref, part_ref, pair_ref, other_ref, one_ref, waves_ref, high_ref, low_ref, *outs):
        even = is_even()
        args = (est_ref, part_ref, pair_ref, other_ref, one_ref, waves_ref, high_ref, low_ref)
        for ref, value in zip(outs, spectrum(even, 1.0 / views, rows, half, *args)):
            ref[...] = value

    return kernel


def cycle_kernel(depth, half):
    def kernel(map_ref, _, cycle_ref):
        columns = jnp.transpose(map_ref[0, :, 0:half].astype(F32))
        cycle = iota((128, CYCLES), 1).astype(F32)
        zero = jnp.zeros((128, 128), BF)
        for k in range(depth // 2 + 1):
            low = columns[:128, k : k + 1] == cycle
            high = columns[128:, k : k + 1] == cycle[:, 128:]
            cycle_ref[pl.ds(k * half, 128), :] = jnp.where(low, 1.0, 0.0).astype(BF)
            cycle_ref[pl.ds(k * half + 128, 128), 0:128] = zero
            cycle_ref[pl.ds(k * half + 128, 128), 128:256] = jnp.where(high, 1.0, 0.0).astype(BF)

    return kernel


def power_kernel(views, slab, depth, lateral, count):
    rows, half = slab * depth, lateral // 2

    def kernel(
        est_ref,
        part_ref,
        pair_ref,
        other_ref,
        one_ref,
        waves_ref,
        high_ref,
        low_ref,
        cycle_ref,
        re_ref,
        im_ref,
        tre_ref,
        tim_ref,
        mre_ref,
        mim_ref,
        mtre_ref,
        mtim_ref,
        sum_ref,
    ):
        even = is_even()
        args = (est_ref, part_ref, pair_ref, other_ref, one_ref, waves_ref, high_ref, low_ref)
        re1, im1, tre1, tim1 = spectrum(even, 1.0 / views, rows, half, *args)
        re0, im0, tre0, tim0 = re_ref[...], im_ref[...], tre_ref[...], tim_ref[...]
        mre_ref[...] = 0.5 * (re0 + re1)
        mim_ref[...] = 0.5 * (im0 + im1)
        mtre_ref[...] = 0.5 * (tre0 + tre1)
        mtim_ref[...] = 0.5 * (tim0 + tim1)

        def over_slab(x):
            total = x[0:depth]
            for s in range(1, slab):
                total = total + x[s * depth : (s + 1) * depth]
            return total

        twice = jnp.where(iota((depth, half), 1) == 0, 1.0, 2.0)
        powers, tops = [], []
        for a, b, c, d in (
            (re0, re1, im0, im1),
            (re0, re0, im0, im0),
            (re1, re1, im1, im1),
        ):
            powers.append(over_slab(a * b + c * d) * twice)
        for a, b, c, d in (
            (tre0, tre1, tim0, tim1),
            (tre0, tre0, tim0, tim0),
            (tre1, tre1, tim1, tim1),
        ):
            tops.append(jnp.sum(over_slab(a * b + c * d), axis=0, keepdims=True))
        top = jnp.sum(jnp.concatenate(tops, axis=0), axis=1, keepdims=True)
        terms = []
        for k in range(depth // 2 + 1):
            other = depth - k
            fold = [p[k : k + 1] + p[other : other + 1] if 0 < k < other else p[k : k + 1] for p in powers]
            terms.append(jnp.concatenate(fold, axis=0))
        term = jnp.concatenate(terms, axis=1)
        high = term.astype(BF).astype(F32)
        middle = (term - high).astype(BF).astype(F32)
        low = term - high - middle
        total = dot(jnp.concatenate([high, middle, low], axis=0).astype(BF), cycle_ref[...])
        last = jnp.where(iota((3, CYCLES), 1) == CYCLES - 1, top, 0.0)
        total = total[0:3] + total[3:6] + total[6:9] + last
        for i in range(count):
            sum_ref[i] = total

    return kernel


def inverse_kernel(slab, depth, lateral, count):
    half = lateral // 2

    def kernel(cut_ref, sum_ref, map_ref, mre_ref, mim_ref, mtre_ref, mtim_ref, back_ref, high_ref, low_ref, out_ref, held, sems):
        total = sum_ref[0]
        for i in range(1, count):
            total = total + sum_ref[i]
        cross, power0, power1 = total[0:1], total[1:2], total[2:3]
        corr = cross / (jnp.sqrt(power0) * jnp.sqrt(power1))
        weight = jnp.where(iota((1, CYCLES), 1) <= cut_ref[0], corr, 0.0)
        low = jnp.broadcast_to(weight[:, 0:128], (depth, 128))
        high = jnp.broadcast_to(weight[:, 128:256], (depth, 128))
        pieces = []
        for j in range(half // 128):
            cell = map_ref[0, :, pl.ds(j * 128, 128)]
            near = cell & 127
            found = jnp.where(
                cell < 128,
                jnp.take_along_axis(low, near, axis=1),
                jnp.take_along_axis(high, near, axis=1),
            )
            twice = jnp.where(iota((depth, 128), 1) + j * 128 == 0, 1.0, 2.0)
            pieces.append(found * twice)
        cells = jnp.concatenate(pieces, axis=1)
        cells = jnp.concatenate([cells] * slab, axis=0)
        last = weight[:, CYCLES - 1 : CYCLES]
        re = mre_ref[...] * cells
        im = mim_ref[...] * cells
        re = jnp.concatenate([re[:, :128] - mtim_ref[...] * last, re[:, 128:]], axis=1)
        im = jnp.concatenate([im[:, :128] + mtre_ref[...] * last, im[:, 128:]], axis=1)
        re_cos, re_sin = z_waves(high_ref[...], low_ref[...], re)
        im_cos, im_sin = z_waves(high_ref[...], low_ref[...], im)
        inner_re = (re_cos - im_sin).astype(BF)
        inner_im = (re_sin + im_cos).astype(BF)
        copies = []
        for j in range(2):
            at = pl.ds(j * half, half)
            joined = dot(inner_re, back_ref[0:half, at]) + dot(inner_im, back_ref[half:lateral, at])
            held[j] = joined * (1.0 / (depth * lateral))
            copies.append(pltpu.make_async_copy(held.at[j], out_ref.at[:, at], sems.at[j]))
            copies[j].start()
        for copy in copies:
            copy.wait()

    return kernel


def body(data_halves, psf_taps, cycle_map, cutoff):
    _, views, slab, depth, lateral = data_halves.shape
    taps = psf_taps.shape[-1]
    radius = taps // 2
    rows, edge = slab * depth, radius * depth
    ext_rows = rows + 2 * edge
    half = lateral // 2
    count = lax.axis_size("tile")
    pairs = [(i, i ^ 1) for i in range(count)]
    others = [(i, i + 1) for i in range(1, count - 1, 2)]
    others = others + [(b, a) for a, b in others]

    def to_other(array):
        return lax.ppermute(array, "tile", others)

    def to_pair(array):
        return lax.ppermute(array, "tile", pairs)

    def exchange(for_pair, for_other):
        other = to_other(for_other)
        return to_pair(for_pair), other

    vmem = pl.BlockSpec(memory_space=pltpu.VMEM)
    scalars = pl.BlockSpec(memory_space=pltpu.SMEM)

    def call(kernel, inputs, outputs, scratch=(), flops=0):
        bytes_moved = sum(int(np.prod(s.shape)) * s.dtype.itemsize for s in outputs)
        return pl.pallas_call(
            kernel,
            in_specs=[scalars if isinstance(x, tuple) else vmem for x in inputs],
            out_specs=tuple(vmem for _ in outputs),
            out_shape=tuple(outputs),
            scratch_shapes=list(scratch),
            cost_estimate=pl.CostEstimate(flops=flops, bytes_accessed=2 * bytes_moved, transcendentals=0),
            compiler_params=pltpu.CompilerParams(vmem_limit_bytes=VMEM_LIMIT),
        )(*[x[0] if isinstance(x, tuple) else x for x in inputs])

    def shaped(*shape, dtype=F32):
        return jax.ShapeDtypeStruct(shape, dtype)

    data = data_halves.reshape(2, views, rows, lateral)
    side = shaped(1, edge, lateral, dtype=BF)
    plane = shaped(rows, lateral)
    begun = call(
        edge_kernel(views, rows, edge),
        [data],
        [plane, shaped(rows, lateral, dtype=BF), shaped(8, 128), side] * 2
        + [shaped(2, edge, lateral, dtype=BF)],
        flops=10**9,
    )
    means, own_exts, levels = begun[0:8:4], begun[1:8:4], begun[2:8:4]
    others0 = [to_other(begun[3]), to_other(begun[7])]
    pair0 = to_pair(begun[8])
    starts = [(pair0, other) for other in others0]

    band = shaped(views, 256, 256, dtype=BF)
    *mats, shape, one0, one1 = call(
        prep_kernel(views, taps, slab, depth, lateral),
        [psf_taps.transpose(1, 0, 2)],
        [
            shaped(views * rows // 2, rows // 2 + 2 * edge, dtype=BF),
            shaped(rows // 2 + 2 * edge, views * rows // 2, dtype=BF),
            band,
            band,
            shaped(2, views * rows, 128),
            shaped(2, views, depth, 128),
            shaped(views, 2, 8, lateral),
            shaped(depth, 128),
            shaped(ext_rows, lateral),
            shaped(rows, lateral),
        ],
        flops=4 * 10**9,
    )

    held = [pltpu.VMEM((2, views * rows // 2, lateral), BF)]
    firsts = []
    for h in range(2):
        own, for_pair, for_other = call(
            first_kernel(h, views, slab, rows, edge),
            [data, own_exts[h], levels[h], *starts[h]] + mats,
            [shaped(rows, lateral)] + [shaped(1, 2 * edge, lateral, dtype=BF)] * 2,
            held,
            flops=4 * 10**9,
        )
        firsts.append((own, for_pair, for_other) + exchange(for_pair, for_other))

    angle = 2.0 * np.pi / lateral * np.arange(256)
    quarter = jnp.asarray(np.cos(angle).astype(np.float32).reshape(2, 128))
    grid_z = np.arange(depth)[:, None] * np.arange(depth)[None, :] % depth * (2.0 * np.pi / depth)
    wave = np.stack([np.cos(grid_z), np.sin(grid_z)]).astype(np.float32)
    wave = jnp.asarray(np.tile(wave, (1, 1, 128 // depth)))
    table = shaped(256, 128, dtype=BF)
    (cycles,) = call(
        cycle_kernel(depth, half),
        [cycle_map, firsts[1][0]],
        [shaped((depth // 2 + 1) * half, CYCLES, dtype=BF)],
        flops=10**9,
    )

    seconds = []
    for h in range(2):
        est, part, for_pair, for_other = call(
            second_kernel(h, views, slab, rows, edge, lateral),
            [data, means[h], levels[h], *starts[h]]
            + [*firsts[h], shape, one0]
            + mats,
            [shaped(rows, lateral)] * 2 + [shaped(1, edge, lateral, dtype=BF)] * 2,
            held,
            flops=4 * 10**9,
        )
        seconds.append((est, part) + exchange(for_pair, for_other))

    waves, back, table_hi, table_lo = call(
        table_kernel(depth, lateral),
        [quarter, wave, seconds[1][0]],
        [shaped(lateral, lateral, dtype=BF), shaped(lateral, lateral, dtype=BF), table, table],
        flops=2 * 10**9,
    )

    plane, top = shaped(rows, half), shaped(rows, 128)
    tables = [one1, waves, table_hi, table_lo]
    spectra = call(
        spectrum_kernel(views, slab, depth, lateral), [*seconds[0]] + tables, [plane, plane, top, top], flops=10**9
    )
    *mixed, sums = call(
        power_kernel(views, slab, depth, lateral, count),
        [*seconds[1]] + tables + [cycles, *spectra],
        [plane, plane, top, top, shaped(count, 3, CYCLES)],
        flops=2 * 10**9,
    )
    sums = lax.all_to_all(sums, "tile", 0, 0)
    joined = pl.pallas_call(
        inverse_kernel(slab, depth, lateral, count),
        in_specs=[scalars] + [vmem] * 9,
        out_specs=pl.BlockSpec(memory_space=pl.ANY),
        out_shape=shaped(rows, lateral),
        scratch_shapes=[pltpu.VMEM((2, rows, half), F32), pltpu.SemaphoreType.DMA((2,))],
        cost_estimate=pl.CostEstimate(flops=10**9, bytes_accessed=10**6, transcendentals=0),
        compiler_params=pltpu.CompilerParams(vmem_limit_bytes=VMEM_LIMIT),
        name="inverse",
    )(cutoff, sums, cycle_map, *mixed, back, table_hi, table_lo)
    return joined.reshape(slab, depth, lateral)


def solution(mesh):
    in_specs = (
        P(None, None, ("groups", "tile"), None, None),
        P(),
        P(("groups", "tile"), None, None),
        P("groups"),
    )
    out_specs = P(("groups", "tile"), None, None)

    return jax.shard_map(body, mesh=mesh, in_specs=in_specs, out_specs=out_specs, check_vma=False)
```

```python
import jax
import jax.numpy as jnp
import numpy as np
from jax import lax
from jax.experimental import pallas as pl
from jax.experimental.pallas import tpu as pltpu
from jax.sharding import PartitionSpec as P


CYCLES = 256
BF = jnp.bfloat16
F32 = jnp.float32
VMEM_LIMIT = 32 * 1024 * 1024


def dot(a, b):
    return lax.dot_general(a, b, (((1,), (0,)), ((), ())), preferred_element_type=F32)


def iota(shape, dim):
    return lax.broadcasted_iota(jnp.int32, shape, dim)


def lookup(index, values):
    total = jnp.zeros(index.shape, F32)
    for place, value in values:
        total = jnp.where(index == place, value, total)
    return total


def shift_rows(x, by):
    count = x.shape[0]
    if by == 0:
        return x
    pad = jnp.zeros((abs(by), x.shape[1]), x.dtype)
    if by > 0:
        return jnp.concatenate([x[by:], pad], axis=0)
    return jnp.concatenate([pad, x[: count + by]], axis=0)


def prep_kernel(later, views, taps, slab, depth, lateral):
    radius = taps // 2
    group = 128 // depth
    ext = slab + 2 * radius
    rows = slab * depth
    scale = 1.0 / views

    def kernel(psf_hbm, *refs):
        kern = psf_hbm
        if not later:
            *refs, kern, sem = refs
            copy = pltpu.make_async_copy(psf_hbm, kern, sem)
            copy.start()
            copy.wait()
            *refs, kept = refs
            kept[...] = kern[...]
        if later:
            held_ref, base_ref, off_ref, w_ref, one0_ref, one1_ref = refs
        else:
            a_ref, b_ref, t_ref, tt_ref, base_ref, off_ref, row_ref = refs
        first = lax.axis_index("tile") * slab
        rows_total = lax.axis_size("tile") * slab

        all_taps = [kern[axis] / jnp.sum(kern[axis], axis=1, keepdims=True) for axis in range(3)]

        def tap(v, axis, t):
            return all_taps[axis][v : v + 1, t : t + 1]

        def spread(x):
            return jnp.concatenate([x] * (depth // 8), axis=0)

        def ones(v, axis, index, count, flip):
            summed = jnp.zeros(index.shape, F32)
            for t in range(taps):
                source = index + t - radius
                ok = (source >= 0) & (source < count)
                summed = summed + jnp.where(ok, tap(v, axis, taps - 1 - t if flip else t), 0.0)
            return summed

        row = iota((depth, 128), 0)
        lane = iota((depth, 128), 1)
        cell = lax.rem(lane, depth)
        slot8 = iota((8, 128), 1) // depth
        gap_z = cell - row + radius
        gap_zt = row - cell + radius
        lane8 = iota((8, 128), 1)
        gap8 = iota((8, 128), 0) - lane8
        zero = jnp.zeros((depth, 128), BF)
        tail = jnp.zeros((120, 128), F32)
        gains = []
        for v in range(0 if later else views):
            band_z = lookup(gap_z, [(t, tap(v, 1, t)) for t in range(taps)])
            band_zt = lookup(gap_zt, [(t, tap(v, 1, t)) for t in range(taps)])

            def lane_taps(shift, sign, v=v):
                pairs = [(j, shift + sign * j) for j in range(group)]
                pairs = [(j, tap(v, 0, t)) for j, t in pairs if 0 <= t < taps]
                return lookup(slot8, pairs) if pairs else None

            blocks = {}
            for i in range(slab // 2):
                for g in range(ext // 2 // group + 1):
                    d = group * g - i
                    if d not in blocks:
                        weight = lane_taps(d, 1)
                        blocks[d] = zero if weight is None else (spread(weight) * band_z).astype(BF)
                    a_ref[pl.ds((v * slab // 2 + i) * depth, depth), pl.ds(g * 128, 128)] = blocks[d]
            for e in range(slab // 2 + 2 * radius):
                block = (spread(lane_taps(e, -1)) * band_zt).astype(BF)
                b_ref[pl.ds(e * depth, depth), pl.ds(v * 128, 128)] = block

            for flip, band_ref in ((False, t_ref), (True, tt_ref)):
                pairs = [(t, tap(v, 2, taps - 1 - t if flip else t)) for t in range(taps)]
                strip = lookup((gap8 + radius) & 127, pairs)
                strips = [strip] + [pltpu.roll(strip, 8 * n, 1) for n in range(1, 16)]
                first_strip = jnp.where(lane8 < 64, strips[0], 0.0)
                last_strip = jnp.where(lane8 >= 64, strips[15], 0.0)
                middle = jnp.concatenate([first_strip] + strips[1:15] + [last_strip], axis=0).astype(BF)
                upper = jnp.concatenate([tail, strips[15] - last_strip], axis=0).astype(BF)
                lower = jnp.concatenate([strips[0] - first_strip, tail], axis=0).astype(BF)
                for at, block in ((0, middle), (1, upper), (2, lower), (3, middle)):
                    at_rows, at_cols = pl.ds(at // 2 * 128, 128), pl.ds(at % 2 * 128, 128)
                    band_ref[v, at_rows, at_cols] = block

            mid = depth // 2
            sum_xz = jnp.sum(
                a_ref[pl.ds(v * rows // 2, depth), :].astype(F32)[mid : mid + 1], axis=1, keepdims=True
            )
            sum_y = jnp.sum(t_ref[v, 0:128, :].astype(F32)[64:65], axis=1, keepdims=True)
            gains.append(1.0 / (sum_xz * sum_y))

        def blur_z(v, x, flip):
            total = None
            for t in range(taps):
                term = shift_rows(x, t - radius) * tap(v, 1, taps - 1 - t if flip else t)
                total = term if total is None else total + term
            return total

        field0 = [ones(v, 1, row, depth, False) for v in range(views)]
        fields = field0
        if later:
            back0 = [blur_z(v, 1.0 / field0[v], True) for v in range(views)]
            shape = back0[0]
            for v in range(1, views):
                shape = shape + back0[v]
            shape = shape * scale
            w_ref[...] = shape
            fields = [blur_z(v, shape, False) for v in range(views)]
            back1 = [blur_z(v, 1.0 / fields[v], True) for v in range(views)]
            gains = [held_ref[v, 1, 0:1, 0:1] for v in range(views)]

        x_out = iota((slab, 128), 0) + first
        x_ext = iota((ext, 128), 0) + (first - radius)
        y_row = iota((8, lateral), 1)
        edges = []
        for v in range(views):
            part_x = ones(v, 0, x_out, rows_total, False)
            for i in range(slab):
                base_ref[pl.ds((v * slab + i) * depth, depth), :] = fields[v] * part_x[i : i + 1]
            off_ref[v] = gains[v] / fields[v]
            if not later:
                row_ref[v, 0] = ones(v, 2, y_row, lateral, False)
                row_ref[v, 1] = jnp.broadcast_to(gains[v], (8, lateral))
                continue
            edges.append((ones(v, 0, x_ext, rows_total, True) * scale, ones(v, 2, y_row, lateral, True)))
        if not later:
            return
        for back, one_ref, low, high in (
            (back0, one0_ref, 0, ext),
            (back1, one1_ref, radius, radius + slab),
        ):
            for e in range(low, high):
                terms = [back[v] * edges[v][0][e : e + 1] for v in range(views)]
                for j in range(lateral // 128):
                    total = None
                    for v in range(views):
                        term = terms[v]
                        if j in (0, lateral // 128 - 1):
                            term = term * edges[v][1][0:1, j * 128 : (j + 1) * 128]
                        total = term if total is None else total + term
                    one_ref[pl.ds((e - low) * depth, depth), pl.ds(j * 128, 128)] = total

    return kernel


def y_blur(x, band):
    rows = x.shape[0]
    stacked = jnp.concatenate([x[:, 0:256], x[:, 128:384], x[:, 256:512]], axis=0)
    wide = dot(stacked, band)
    left, mid, right = wide[:rows], wide[rows : 2 * rows], wide[2 * rows :]
    low = iota((rows, 128), 1) < 64
    return jnp.concatenate(
        [
            left[:, :128],
            jnp.where(low, left[:, 128:], mid[:, :128]),
            jnp.where(low, mid[:, 128:], right[:, :128]),
            right[:, 128:],
        ],
        axis=1,
    )


def level_of(x):
    total = jnp.sum(jnp.sum(x, axis=0, keepdims=True), axis=1, keepdims=True)
    return (total * (1.0 / x.size)).astype(BF).astype(F32)


def across(x, lateral):
    return jnp.concatenate([x] * (lateral // 128), axis=1)


def blur_back(views, slab, rows, level, data_ref, ext, mats, held):
    a_ref, b_ref, t_ref, tt_ref, base_ref, off_ref, row_ref = mats
    lateral = ext.shape[1]
    half = rows // 2
    seen = a_ref.shape[1]
    held[0] = dot(a_ref[...], ext[:seen]).astype(BF)
    held[1] = dot(a_ref[...], ext[half:]).astype(BF)
    for v in range(views):
        at = pl.ds(v * half, half)
        part = jnp.concatenate([held[0, at, :], held[1, at, :]], axis=0)
        base = across(base_ref[pl.ds(v * rows, rows), :], lateral) * (row_ref[v, 0, 0:1, :] * level)
        predicted = y_blur(part, t_ref[v]) + base
        scaled = data_ref[v].astype(F32) * row_ref[v, 1, 0:1, :]
        offset = across(jnp.concatenate([off_ref[v]] * slab, axis=0), lateral)
        quotient = (scaled / predicted - offset).astype(BF)
        back = y_blur(quotient, tt_ref[v]).astype(BF)
        held[0, at, :] = back[:half]
        held[1, at, :] = back[half:]
    low = dot(b_ref[...], held[0])
    high = dot(b_ref[...], held[1])
    return jnp.concatenate([low[:half], low[half:] + high[: seen - half], high[seen - half :]], axis=0)


def pick(even, from_pair, from_other, h=0):
    pair = from_pair[h].astype(F32)
    other = from_other[0].astype(F32)
    return jnp.where(even, other, pair), jnp.where(even, pair, other)


def put(even, low, high, to_pair, to_other, h=0, g=0):
    to_pair[h] = jnp.where(even, high, low).astype(BF)
    to_other[g] = jnp.where(even, low, high).astype(BF)


def is_even():
    return (lax.axis_index("tile") & 1) == 0


def has_sides():
    index = lax.axis_index("tile")
    return jnp.where(index > 0, 1.0, 0.0), jnp.where(index + 1 < lax.axis_size("tile"), 1.0, 0.0)


def mean_views(h, data_ref, views):
    total = data_ref[h, 0].astype(F32)
    for v in range(1, views):
        total = total + data_ref[h, v].astype(F32)
    return total * (1.0 / views)


def edge_kernel(views, rows, edge):
    def kernel(data_ref, *outs):
        even = is_even()
        to_pair = outs[-1]
        for h in range(2):
            est_ref, ext_ref, level_ref, to_other = outs[4 * h : 4 * h + 4]
            est = mean_views(h, data_ref, views)
            est_ref[...] = est
            put(even, est[:edge], est[rows - edge :], to_pair, to_other, h, 0)
            level = level_of(est)
            ext_ref[...] = (est - level).astype(BF)
            level_ref[...] = jnp.broadcast_to(level, level_ref.shape)

    return kernel


def first_kernel(h, views, slab, rows, edge):
    def kernel(data_ref, own_ext, level_ref, pair_ref, other_ref, *refs):
        mats, (own_ref, to_pair, to_other, held) = refs[:7], refs[7:]
        even = is_even()
        lo, hi = pick(even, pair_ref, other_ref, h)
        has_lo, has_hi = has_sides()
        level = level_ref[0:1, 0:1]
        lo = (lo - level * has_lo).astype(BF)
        hi = (hi - level * has_hi).astype(BF)
        ext = jnp.concatenate([lo, own_ext[...], hi], axis=0)
        part = blur_back(views, slab, rows, level, data_ref.at[h], ext, mats, held)
        own_ref[...] = part[edge : edge + rows]
        put(even, part[0 : 2 * edge], part[rows:], to_pair, to_other)

    return kernel


def second_kernel(h, views, slab, rows, edge, lateral):
    scale = 1.0 / views

    def kernel(
        data_ref, start_ref, level_ref, pair0_ref, other0_ref, own_ref, sent_pair, sent_other, pair_ref, other_ref, w_ref, one_ref, *refs
    ):
        mats, (est_ref, part_ref, to_pair, to_other, held) = refs[:7], refs[7:]
        even = is_even()
        has_lo, has_hi = has_sides()
        lo, hi = pick(even, pair0_ref, other0_ref, h)
        got_lo, got_hi = pick(even, pair_ref, other_ref)
        sent_lo, sent_hi = pick(even, sent_pair, sent_other)
        lo = lo * (one_ref[0:edge] + scale * (sent_lo[0:edge] + got_lo[0:edge]))
        hi = hi * (one_ref[edge + rows :] + scale * (sent_hi[edge:] + got_hi[edge:]))
        got = jnp.concatenate([got_lo[edge:], got_hi[0:edge]], axis=0)
        level = level_ref[0:1, 0:1]
        estimate = start_ref[...] * (one_ref[pl.ds(edge, rows)] + scale * (own_ref[...] + got))
        est_ref[...] = estimate
        shape = across(w_ref[...], lateral) * level
        shapes = jnp.concatenate([shape] * (edge // shape.shape[0]), axis=0)
        ext = jnp.concatenate(
            [
                lo - shapes * has_lo,
                estimate - jnp.concatenate([shape] * slab, axis=0),
                hi - shapes * has_hi,
            ],
            axis=0,
        )
        part = blur_back(views, slab, rows, level, data_ref.at[h], ext.astype(BF), mats, held)
        part_ref[...] = part[edge : edge + rows]
        put(even, part[0:edge], part[edge + rows :], to_pair, to_other)

    return kernel


def table_kernel(depth, lateral):
    half = lateral // 2

    def kernel(quarter_ref, wave_ref, _, waves_ref, back_ref, high_ref, low_ref):
        steps = [jnp.broadcast_to(quarter_ref[0:1, :], (8, 128)), jnp.broadcast_to(quarter_ref[1:2, :], (8, 128))]
        row8 = iota((8, 128), 0)
        odd_row = (iota((16, 128), 0) & 1) == 1
        odd_lane = (iota((16, 128), 1) & 1) == 1
        for j in range(half // 128):
            lane = iota((8, 128), 1) + j * 128
            phase = (row8 * lane) & (lateral - 1)
            for i in range(half // 16):
                pair = []
                for _ in range(2):
                    near, turn = phase & 127, phase // 128
                    g0 = jnp.take_along_axis(steps[0], near, axis=1)
                    g1 = jnp.take_along_axis(steps[1], near, axis=1)
                    odd = (turn & 1) == 1
                    cos = jnp.where(odd, g1, g0)
                    sin = jnp.where(odd, g0, g1)
                    pair.append((jnp.where(turn >= 2, -cos, cos), jnp.where((turn == 0) | (turn == 3), -sin, sin)))
                    phase = (phase + lane * 8) & (lateral - 1)
                cos = jnp.concatenate([pair[0][0], pair[1][0]], axis=0)
                sin = jnp.concatenate([pair[0][1], pair[1][1]], axis=0)
                ahead, behind = sin, -sin
                if j == 0:
                    ahead = jnp.where(iota((16, 128), 1) == 0, jnp.where(odd_row, -1.0, 1.0), sin)
                if i == 0:
                    behind = jnp.where(iota((16, 128), 0) == 0, jnp.where(odd_lane, -1.0, 1.0), behind)
                here, there = pl.ds(i * 16, 16), pl.ds(half + i * 16, 16)
                left, right = pl.ds(j * 128, 128), pl.ds(half + j * 128, 128)
                waves_ref[here, left] = cos.astype(BF)
                waves_ref[here, right] = ahead.astype(BF)
                waves_ref[there, left] = jnp.where(odd_lane, -cos, cos).astype(BF)
                waves_ref[there, right] = jnp.where(odd_lane, -ahead, ahead).astype(BF)
                back_ref[here, left] = cos.astype(BF)
                back_ref[here, right] = jnp.where(odd_row, -cos, cos).astype(BF)
                back_ref[there, left] = behind.astype(BF)
                back_ref[there, right] = jnp.where(odd_row, -behind, behind).astype(BF)
        slot = iota((depth, 128), 1) // depth
        group = 128 // depth
        for kind in range(2):
            wave = wave_ref[kind]
            high = wave.astype(BF).astype(F32)
            for i in range(group):
                at = pl.ds((kind * group + i) * depth, depth)
                here = slot == i
                high_ref[at, :] = jnp.where(here, high, 0.0).astype(BF)
                low_ref[at, :] = jnp.where(here, wave - high, 0.0).astype(BF)

    return kernel


def z_waves(table_hi, table_lo, x):
    cosines, sines = [], []
    for at in range(0, x.shape[0], 128):
        part = x[at : at + 128]
        high = part.astype(BF)
        low = (part - high.astype(F32)).astype(BF)
        total = dot(table_hi, high) + dot(table_hi, low) + dot(table_lo, high)
        cosines.append(total[:128])
        sines.append(total[128:])
    return jnp.concatenate(cosines, axis=0), jnp.concatenate(sines, axis=0)


def spectrum(even, scale, rows, half, est_ref, part_ref, pair_ref, other_ref, one_ref, waves_ref, high_ref, low_ref):
    got_lo, got_hi = pick(even, pair_ref, other_ref)
    got = jnp.concatenate([got_lo, got_hi], axis=0)
    estimate = est_ref[...] * (one_ref[...] + scale * (part_ref[...] + got))
    row = dot(estimate.astype(BF), waves_ref[...])
    cos_cos, cos_sin = z_waves(high_ref[...], low_ref[...], row[:, :half])
    sin_cos, sin_sin = z_waves(high_ref[...], low_ref[...], row[:, half:])
    first = iota((rows, half), 1) == 0
    real = cos_cos - jnp.where(first, 0.0, sin_sin)
    imag = -cos_sin - jnp.where(first, 0.0, sin_cos)
    top = iota((rows, 128), 1) == 0
    top_real = jnp.where(top, sin_cos[:, :128], 0.0)
    top_imag = jnp.where(top, -sin_sin[:, :128], 0.0)
    return real, imag, top_real, top_imag


def spectrum_kernel(views, slab, depth, lateral):
    rows, half = slab * depth, lateral // 2

    def kernel(est_ref, part_ref, pair_ref, other_ref, one_ref, waves_ref, high_ref, low_ref, *outs):
        even = is_even()
        args = (est_ref, part_ref, pair_ref, other_ref, one_ref, waves_ref, high_ref, low_ref)
        for ref, value in zip(outs, spectrum(even, 1.0 / views, rows, half, *args)):
            ref[...] = value

    return kernel


def cycle_kernel(depth, half):
    def kernel(map_ref, _, cycle_ref):
        columns = jnp.transpose(map_ref[0, :, 0:half].astype(F32))
        cycle = iota((128, CYCLES), 1).astype(F32)
        zero = jnp.zeros((128, 128), BF)
        for k in range(depth // 2 + 1):
            low = columns[:128, k : k + 1] == cycle
            high = columns[128:, k : k + 1] == cycle[:, 128:]
            cycle_ref[pl.ds(k * half, 128), :] = jnp.where(low, 1.0, 0.0).astype(BF)
            cycle_ref[pl.ds(k * half + 128, 128), 0:128] = zero
            cycle_ref[pl.ds(k * half + 128, 128), 128:256] = jnp.where(high, 1.0, 0.0).astype(BF)

    return kernel


def power_kernel(views, slab, depth, lateral, count):
    rows, half = slab * depth, lateral // 2

    def kernel(
        est_ref,
        part_ref,
        pair_ref,
        other_ref,
        one_ref,
        waves_ref,
        high_ref,
        low_ref,
        cycle_ref,
        re_ref,
        im_ref,
        tre_ref,
        tim_ref,
        mre_ref,
        mim_ref,
        mtre_ref,
        mtim_ref,
        sum_ref,
    ):
        even = is_even()
        args = (est_ref, part_ref, pair_ref, other_ref, one_ref, waves_ref, high_ref, low_ref)
        re1, im1, tre1, tim1 = spectrum(even, 1.0 / views, rows, half, *args)
        re0, im0, tre0, tim0 = re_ref[...], im_ref[...], tre_ref[...], tim_ref[...]
        mre_ref[...] = 0.5 * (re0 + re1)
        mim_ref[...] = 0.5 * (im0 + im1)
        mtre_ref[...] = 0.5 * (tre0 + tre1)
        mtim_ref[...] = 0.5 * (tim0 + tim1)

        def over_slab(x):
            total = x[0:depth]
            for s in range(1, slab):
                total = total + x[s * depth : (s + 1) * depth]
            return total

        twice = jnp.where(iota((depth, half), 1) == 0, 1.0, 2.0)
        powers, tops = [], []
        for a, b, c, d in (
            (re0, re1, im0, im1),
            (re0, re0, im0, im0),
            (re1, re1, im1, im1),
        ):
            powers.append(over_slab(a * b + c * d) * twice)
        for a, b, c, d in (
            (tre0, tre1, tim0, tim1),
            (tre0, tre0, tim0, tim0),
            (tre1, tre1, tim1, tim1),
        ):
            tops.append(jnp.sum(over_slab(a * b + c * d), axis=0, keepdims=True))
        top = jnp.sum(jnp.concatenate(tops, axis=0), axis=1, keepdims=True)
        terms = []
        for k in range(depth // 2 + 1):
            other = depth - k
            fold = [p[k : k + 1] + p[other : other + 1] if 0 < k < other else p[k : k + 1] for p in powers]
            terms.append(jnp.concatenate(fold, axis=0))
        term = jnp.concatenate(terms, axis=1)
        high = term.astype(BF).astype(F32)
        middle = (term - high).astype(BF).astype(F32)
        low = term - high - middle
        total = dot(jnp.concatenate([high, middle, low], axis=0).astype(BF), cycle_ref[...])
        last = jnp.where(iota((3, CYCLES), 1) == CYCLES - 1, top, 0.0)
        total = total[0:3] + total[3:6] + total[6:9] + last
        for i in range(count):
            sum_ref[i] = total

    return kernel


def inverse_kernel(slab, depth, lateral, count):
    half = lateral // 2

    def kernel(cut_ref, sum_ref, map_ref, mre_ref, mim_ref, mtre_ref, mtim_ref, back_ref, high_ref, low_ref, out_ref, held, sems):
        total = sum_ref[0]
        for i in range(1, count):
            total = total + sum_ref[i]
        cross, power0, power1 = total[0:1], total[1:2], total[2:3]
        corr = cross / (jnp.sqrt(power0) * jnp.sqrt(power1))
        weight = jnp.where(iota((1, CYCLES), 1) <= cut_ref[0], corr, 0.0)
        low = jnp.broadcast_to(weight[:, 0:128], (depth, 128))
        high = jnp.broadcast_to(weight[:, 128:256], (depth, 128))
        pieces = []
        for j in range(half // 128):
            cell = map_ref[0, :, pl.ds(j * 128, 128)]
            near = cell & 127
            found = jnp.where(
                cell < 128,
                jnp.take_along_axis(low, near, axis=1),
                jnp.take_along_axis(high, near, axis=1),
            )
            twice = jnp.where(iota((depth, 128), 1) + j * 128 == 0, 1.0, 2.0)
            pieces.append(found * twice)
        cells = jnp.concatenate(pieces, axis=1)
        cells = jnp.concatenate([cells] * slab, axis=0)
        last = weight[:, CYCLES - 1 : CYCLES]
        re = mre_ref[...] * cells
        im = mim_ref[...] * cells
        re = jnp.concatenate([re[:, :128] - mtim_ref[...] * last, re[:, 128:]], axis=1)
        im = jnp.concatenate([im[:, :128] + mtre_ref[...] * last, im[:, 128:]], axis=1)
        re_cos, re_sin = z_waves(high_ref[...], low_ref[...], re)
        im_cos, im_sin = z_waves(high_ref[...], low_ref[...], im)
        inner_re = (re_cos - im_sin).astype(BF)
        inner_im = (re_sin + im_cos).astype(BF)
        copies = []
        for j in range(2):
            at = pl.ds(j * half, half)
            joined = dot(inner_re, back_ref[0:half, at]) + dot(inner_im, back_ref[half:lateral, at])
            held[j] = joined * (1.0 / (depth * lateral))
            copies.append(pltpu.make_async_copy(held.at[j], out_ref.at[:, at], sems.at[j]))
            copies[j].start()
        for copy in copies:
            copy.wait()

    return kernel


def body(data_halves, psf_taps, cycle_map, cutoff):
    _, views, slab, depth, lateral = data_halves.shape
    taps = psf_taps.shape[-1]
    radius = taps // 2
    rows, edge = slab * depth, radius * depth
    ext_rows = rows + 2 * edge
    half = lateral // 2
    count = lax.axis_size("tile")
    pairs = [(i, i ^ 1) for i in range(count)]
    others = [(i, i + 1) for i in range(1, count - 1, 2)]
    others = others + [(b, a) for a, b in others]

    def to_other(array):
        return lax.ppermute(array, "tile", others)

    def to_pair(array):
        return lax.ppermute(array, "tile", pairs)

    def exchange(for_pair, for_other):
        other = to_other(for_other)
        return to_pair(for_pair), other

    vmem = pl.BlockSpec(memory_space=pltpu.VMEM)
    scalars = pl.BlockSpec(memory_space=pltpu.SMEM)

    def call(kernel, inputs, outputs, scratch=(), flops=0):
        bytes_moved = sum(int(np.prod(s.shape)) * s.dtype.itemsize for s in outputs)
        return pl.pallas_call(
            kernel,
            in_specs=[x[1] if isinstance(x, tuple) else vmem for x in inputs],
            out_specs=tuple(vmem for _ in outputs),
            out_shape=tuple(outputs),
            scratch_shapes=list(scratch),
            cost_estimate=pl.CostEstimate(flops=flops, bytes_accessed=2 * bytes_moved, transcendentals=0),
            compiler_params=pltpu.CompilerParams(vmem_limit_bytes=VMEM_LIMIT),
        )(*[x[0] if isinstance(x, tuple) else x for x in inputs])

    def shaped(*shape, dtype=F32):
        return jax.ShapeDtypeStruct(shape, dtype)

    data = data_halves.reshape(2, views, rows, lateral)
    side = shaped(1, edge, lateral, dtype=BF)
    plane = shaped(rows, lateral)
    begun = call(
        edge_kernel(views, rows, edge),
        [data],
        [plane, shaped(rows, lateral, dtype=BF), shaped(8, 128), side] * 2
        + [shaped(2, edge, lateral, dtype=BF)],
        flops=10**9,
    )
    means, own_exts, levels = begun[0:8:4], begun[1:8:4], begun[2:8:4]
    others0 = [to_other(begun[3]), to_other(begun[7])]
    pair0 = to_pair(begun[8])
    starts = [(pair0, other) for other in others0]

    band = shaped(views, 256, 256, dtype=BF)
    base, offset = shaped(views * rows, 128), shaped(views, depth, 128)
    psf = pltpu.with_memory_space_constraint(psf_taps.transpose(1, 0, 2), pltpu.HBM)
    psf = (psf, pl.BlockSpec(memory_space=pltpu.HBM))
    taps_here = [pltpu.VMEM((3, views, taps), F32), pltpu.SemaphoreType.DMA]
    *mats, kept = call(
        prep_kernel(False, views, taps, slab, depth, lateral),
        [psf],
        [
            shaped(views * rows // 2, rows // 2 + 2 * edge, dtype=BF),
            shaped(rows // 2 + 2 * edge, views * rows // 2, dtype=BF),
            band,
            band,
            base,
            offset,
            shaped(views, 2, 8, lateral),
            shaped(3, views, taps),
        ],
        taps_here,
        flops=4 * 10**9,
    )
    base1, offset1, shape, one0, one1 = call(
        prep_kernel(True, views, taps, slab, depth, lateral),
        [kept, mats[6]],
        [base, offset, shaped(depth, 128), shaped(ext_rows, lateral), shaped(rows, lateral)],
        flops=10**9,
    )
    mats1 = [*mats[:4], base1, offset1, mats[6]]

    held = [pltpu.VMEM((2, views * rows // 2, lateral), BF)]
    firsts = []
    for h in range(2):
        own, for_pair, for_other = call(
            first_kernel(h, views, slab, rows, edge),
            [data, own_exts[h], levels[h], *starts[h], *mats],
            [shaped(rows, lateral)] + [shaped(1, 2 * edge, lateral, dtype=BF)] * 2,
            held,
            flops=4 * 10**9,
        )
        firsts.append((own, for_pair, for_other) + exchange(for_pair, for_other))

    angle = 2.0 * np.pi / lateral * np.arange(256)
    quarter = jnp.asarray(np.cos(angle).astype(np.float32).reshape(2, 128))
    grid_z = np.arange(depth)[:, None] * np.arange(depth)[None, :] % depth * (2.0 * np.pi / depth)
    wave = np.stack([np.cos(grid_z), np.sin(grid_z)]).astype(np.float32)
    wave = jnp.asarray(np.tile(wave, (1, 1, 128 // depth)))
    table = shaped(256, 128, dtype=BF)
    seconds = []
    for h in range(2):
        est, part, for_pair, for_other = call(
            second_kernel(h, views, slab, rows, edge, lateral),
            [data, means[h], levels[h], *starts[h]]
            + [*firsts[h], shape, one0]
            + mats1,
            [shaped(rows, lateral)] * 2 + [shaped(1, edge, lateral, dtype=BF)] * 2,
            held,
            flops=4 * 10**9,
        )
        seconds.append((est, part) + exchange(for_pair, for_other))

    waves, back, table_hi, table_lo = call(
        table_kernel(depth, lateral),
        [quarter, wave, seconds[1][0]],
        [shaped(lateral, lateral, dtype=BF), shaped(lateral, lateral, dtype=BF), table, table],
        flops=2 * 10**9,
    )

    (cycles,) = call(
        cycle_kernel(depth, half),
        [cycle_map, seconds[1][0]],
        [shaped((depth // 2 + 1) * half, CYCLES, dtype=BF)],
        flops=10**9,
    )

    plane, top = shaped(rows, half), shaped(rows, 128)
    tables = [one1, waves, table_hi, table_lo]
    spectra = call(
        spectrum_kernel(views, slab, depth, lateral), [*seconds[0]] + tables, [plane, plane, top, top], flops=10**9
    )
    *mixed, sums = call(
        power_kernel(views, slab, depth, lateral, count),
        [*seconds[1]] + tables + [cycles, *spectra],
        [plane, plane, top, top, shaped(count, 3, CYCLES)],
        flops=2 * 10**9,
    )
    sums = lax.all_to_all(sums, "tile", 0, 0)
    joined = pl.pallas_call(
        inverse_kernel(slab, depth, lateral, count),
        in_specs=[scalars] + [vmem] * 9,
        out_specs=pl.BlockSpec(memory_space=pl.ANY),
        out_shape=shaped(rows, lateral),
        scratch_shapes=[pltpu.VMEM((2, rows, half), F32), pltpu.SemaphoreType.DMA((2,))],
        cost_estimate=pl.CostEstimate(flops=10**9, bytes_accessed=10**6, transcendentals=0),
        compiler_params=pltpu.CompilerParams(vmem_limit_bytes=VMEM_LIMIT),
        name="inverse",
    )(cutoff, sums, cycle_map, *mixed, back, table_hi, table_lo)
    return joined.reshape(slab, depth, lateral)


def solution(mesh):
    in_specs = (
        P(None, None, ("groups", "tile"), None, None),
        P(),
        P(("groups", "tile"), None, None),
        P("groups"),
    )
    out_specs = P(("groups", "tile"), None, None)

    return jax.shard_map(body, mesh=mesh, in_specs=in_specs, out_specs=out_specs, check_vma=False)
```

```python
import jax
import jax.numpy as jnp
import numpy as np
from jax import lax
from jax.experimental import pallas as pl
from jax.experimental.pallas import tpu as pltpu
from jax.sharding import PartitionSpec as P


CYCLES = 256
BF = jnp.bfloat16
F32 = jnp.float32
VMEM_LIMIT = 32 * 1024 * 1024


def dot(a, b):
    return lax.dot_general(a, b, (((1,), (0,)), ((), ())), preferred_element_type=F32)


def iota(shape, dim):
    return lax.broadcasted_iota(jnp.int32, shape, dim)


def lookup(index, values):
    total = jnp.zeros(index.shape, F32)
    for place, value in values:
        total = jnp.where(index == place, value, total)
    return total


def shift_rows(x, by):
    count = x.shape[0]
    if by == 0:
        return x
    pad = jnp.zeros((abs(by), x.shape[1]), x.dtype)
    if by > 0:
        return jnp.concatenate([x[by:], pad], axis=0)
    return jnp.concatenate([pad, x[: count + by]], axis=0)


def prep_kernel(later, views, taps, slab, depth, lateral):
    radius = taps // 2
    group = 128 // depth
    ext = slab + 2 * radius
    rows = slab * depth
    scale = 1.0 / views

    def kernel(psf_hbm, *refs):
        kern = psf_hbm
        if not later:
            *refs, kern, sem = refs
            copy = pltpu.make_async_copy(psf_hbm, kern, sem)
            copy.start()
            copy.wait()
            *refs, kept = refs
            kept[...] = kern[...]
        if later:
            held_ref, base_ref, off_ref, w_ref, one0_ref, one1_ref = refs
        else:
            a_ref, b_ref, t_ref, tt_ref, base_ref, off_ref, row_ref = refs
        first = lax.axis_index("tile") * slab
        rows_total = lax.axis_size("tile") * slab

        all_taps = [kern[axis] / jnp.sum(kern[axis], axis=1, keepdims=True) for axis in range(3)]

        def tap(v, axis, t):
            return all_taps[axis][v : v + 1, t : t + 1]

        def spread(x):
            return jnp.concatenate([x] * (depth // 8), axis=0)

        def ones(v, axis, index, count, flip):
            summed = jnp.zeros(index.shape, F32)
            for t in range(taps):
                source = index + t - radius
                ok = (source >= 0) & (source < count)
                summed = summed + jnp.where(ok, tap(v, axis, taps - 1 - t if flip else t), 0.0)
            return summed

        row = iota((depth, 128), 0)
        lane = iota((depth, 128), 1)
        cell = lax.rem(lane, depth)
        slot8 = iota((8, 128), 1) // depth
        gap_z = cell - row + radius
        gap_zt = row - cell + radius
        lane8 = iota((8, 128), 1)
        gap8 = iota((8, 128), 0) - lane8
        zero = jnp.zeros((depth, 128), BF)
        tail = jnp.zeros((120, 128), F32)
        gains = []
        for v in range(0 if later else views):
            band_z = lookup(gap_z, [(t, tap(v, 1, t)) for t in range(taps)])
            band_zt = lookup(gap_zt, [(t, tap(v, 1, t)) for t in range(taps)])

            def lane_taps(shift, sign, v=v):
                pairs = [(j, shift + sign * j) for j in range(group)]
                pairs = [(j, tap(v, 0, t)) for j, t in pairs if 0 <= t < taps]
                return lookup(slot8, pairs) if pairs else None

            blocks = {}
            for i in range(slab // 2):
                for g in range(ext // 2 // group + 1):
                    d = group * g - i
                    if d not in blocks:
                        weight = lane_taps(d, 1)
                        blocks[d] = zero if weight is None else (spread(weight) * band_z).astype(BF)
                    a_ref[pl.ds((v * slab // 2 + i) * depth, depth), pl.ds(g * 128, 128)] = blocks[d]
            for e in range(slab // 2 + 2 * radius):
                block = (spread(lane_taps(e, -1)) * band_zt).astype(BF)
                b_ref[pl.ds(e * depth, depth), pl.ds(v * 128, 128)] = block

            for flip, band_ref in ((False, t_ref), (True, tt_ref)):
                pairs = [(t, tap(v, 2, taps - 1 - t if flip else t)) for t in range(taps)]
                strip = lookup((gap8 + radius) & 127, pairs)
                strips = [strip] + [pltpu.roll(strip, 8 * n, 1) for n in range(1, 16)]
                first_strip = jnp.where(lane8 < 64, strips[0], 0.0)
                last_strip = jnp.where(lane8 >= 64, strips[15], 0.0)
                middle = jnp.concatenate([first_strip] + strips[1:15] + [last_strip], axis=0).astype(BF)
                upper = jnp.concatenate([tail, strips[15] - last_strip], axis=0).astype(BF)
                lower = jnp.concatenate([strips[0] - first_strip, tail], axis=0).astype(BF)
                for at, block in ((0, middle), (1, upper), (2, lower), (3, middle)):
                    at_rows, at_cols = pl.ds(at // 2 * 128, 128), pl.ds(at % 2 * 128, 128)
                    band_ref[v, at_rows, at_cols] = block

            mid = depth // 2
            sum_xz = jnp.sum(
                a_ref[pl.ds(v * rows // 2, depth), :].astype(F32)[mid : mid + 1], axis=1, keepdims=True
            )
            sum_y = jnp.sum(t_ref[v, 0:128, :].astype(F32)[64:65], axis=1, keepdims=True)
            gains.append(1.0 / (sum_xz * sum_y))

        def blur_z(v, x, flip):
            total = None
            for t in range(taps):
                term = shift_rows(x, t - radius) * tap(v, 1, taps - 1 - t if flip else t)
                total = term if total is None else total + term
            return total

        field0 = [ones(v, 1, row, depth, False) for v in range(views)]
        fields = field0
        if later:
            back0 = [blur_z(v, 1.0 / field0[v], True) for v in range(views)]
            shape = back0[0]
            for v in range(1, views):
                shape = shape + back0[v]
            shape = shape * scale
            w_ref[...] = shape
            fields = [blur_z(v, shape, False) for v in range(views)]
            back1 = [blur_z(v, 1.0 / fields[v], True) for v in range(views)]
            gains = [held_ref[v, 1, 0:1, 0:1] for v in range(views)]

        x_out = iota((slab, 128), 0) + first
        x_ext = iota((ext, 128), 0) + (first - radius)
        y_row = iota((8, lateral), 1)
        edges = []
        for v in range(views):
            part_x = ones(v, 0, x_out, rows_total, False)
            for i in range(slab):
                base_ref[pl.ds((v * slab + i) * depth, depth), :] = fields[v] * part_x[i : i + 1]
            off_ref[v] = gains[v] / fields[v]
            if not later:
                row_ref[v, 0] = ones(v, 2, y_row, lateral, False)
                row_ref[v, 1] = jnp.broadcast_to(gains[v], (8, lateral))
                continue
            edges.append((ones(v, 0, x_ext, rows_total, True) * scale, ones(v, 2, y_row, lateral, True)))
        if not later:
            return
        for back, one_ref, low, high in (
            (back0, one0_ref, 0, ext),
            (back1, one1_ref, radius, radius + slab),
        ):
            for e in range(low, high):
                terms = [back[v] * edges[v][0][e : e + 1] for v in range(views)]
                for j in range(lateral // 128):
                    total = None
                    for v in range(views):
                        term = terms[v]
                        if j in (0, lateral // 128 - 1):
                            term = term * edges[v][1][0:1, j * 128 : (j + 1) * 128]
                        total = term if total is None else total + term
                    one_ref[pl.ds((e - low) * depth, depth), pl.ds(j * 128, 128)] = total

    return kernel


def y_blur(x, band):
    rows = x.shape[0]
    stacked = jnp.concatenate([x[:, 0:256], x[:, 128:384], x[:, 256:512]], axis=0)
    wide = dot(stacked, band)
    left, mid, right = wide[:rows], wide[rows : 2 * rows], wide[2 * rows :]
    low = iota((rows, 128), 1) < 64
    return jnp.concatenate(
        [
            left[:, :128],
            jnp.where(low, left[:, 128:], mid[:, :128]),
            jnp.where(low, mid[:, 128:], right[:, :128]),
            right[:, 128:],
        ],
        axis=1,
    )


def level_of(x):
    total = jnp.sum(jnp.sum(x, axis=0, keepdims=True), axis=1, keepdims=True)
    return (total * (1.0 / x.size)).astype(BF).astype(F32)


def across(x, lateral):
    return jnp.concatenate([x] * (lateral // 128), axis=1)


def blur_back(views, slab, rows, level, data_ref, ext, mats, held):
    a_ref, b_ref, t_ref, tt_ref, base_ref, off_ref, row_ref = mats
    lateral = ext.shape[1]
    half = rows // 2
    seen = a_ref.shape[1]
    held[0] = dot(a_ref[...], ext[:seen]).astype(BF)
    held[1] = dot(a_ref[...], ext[half:]).astype(BF)
    for v in range(views):
        at = pl.ds(v * half, half)
        part = jnp.concatenate([held[0, at, :], held[1, at, :]], axis=0)
        base = across(base_ref[pl.ds(v * rows, rows), :], lateral) * (row_ref[v, 0, 0:1, :] * level)
        predicted = y_blur(part, t_ref[v]) + base
        scaled = data_ref[v].astype(F32) * row_ref[v, 1, 0:1, :]
        offset = across(jnp.concatenate([off_ref[v]] * slab, axis=0), lateral)
        quotient = (scaled / predicted - offset).astype(BF)
        back = y_blur(quotient, tt_ref[v]).astype(BF)
        held[0, at, :] = back[:half]
        held[1, at, :] = back[half:]
    low = dot(b_ref[...], held[0])
    high = dot(b_ref[...], held[1])
    return jnp.concatenate([low[:half], low[half:] + high[: seen - half], high[seen - half :]], axis=0)


def pick(even, from_pair, from_other, h=0):
    pair = from_pair[h].astype(F32)
    other = from_other[0].astype(F32)
    return jnp.where(even, other, pair), jnp.where(even, pair, other)


def put(even, low, high, to_pair, to_other, h=0, g=0):
    to_pair[h] = jnp.where(even, high, low).astype(BF)
    to_other[g] = jnp.where(even, low, high).astype(BF)


def is_even():
    return (lax.axis_index("tile") & 1) == 0


def has_sides():
    index = lax.axis_index("tile")
    return jnp.where(index > 0, 1.0, 0.0), jnp.where(index + 1 < lax.axis_size("tile"), 1.0, 0.0)


def mean_views(h, data_ref, views):
    total = data_ref[h, 0].astype(F32)
    for v in range(1, views):
        total = total + data_ref[h, v].astype(F32)
    return total * (1.0 / views)


def edge_kernel(views, rows, edge):
    def kernel(data_ref, *outs):
        even = is_even()
        to_pair = outs[-1]
        for h in range(2):
            est_ref, ext_ref, level_ref, to_other = outs[4 * h : 4 * h + 4]
            est = mean_views(h, data_ref, views)
            est_ref[...] = est
            put(even, est[:edge], est[rows - edge :], to_pair, to_other, h, 0)
            level = level_of(est)
            ext_ref[...] = (est - level).astype(BF)
            level_ref[...] = jnp.broadcast_to(level, level_ref.shape)

    return kernel


def first_kernel(h, views, slab, rows, edge):
    def kernel(data_ref, own_ext, level_ref, pair_ref, other_ref, *refs):
        mats, (own_ref, to_pair, to_other, held) = refs[:7], refs[7:]
        even = is_even()
        lo, hi = pick(even, pair_ref, other_ref, h)
        has_lo, has_hi = has_sides()
        level = level_ref[0:1, 0:1]
        lo = (lo - level * has_lo).astype(BF)
        hi = (hi - level * has_hi).astype(BF)
        ext = jnp.concatenate([lo, own_ext[...], hi], axis=0)
        part = blur_back(views, slab, rows, level, data_ref.at[h], ext, mats, held)
        own_ref[...] = part[edge : edge + rows]
        put(even, part[0 : 2 * edge], part[rows:], to_pair, to_other)

    return kernel


def second_kernel(h, views, slab, rows, edge, lateral):
    scale = 1.0 / views

    def kernel(
        data_ref, start_ref, level_ref, pair0_ref, other0_ref, own_ref, sent_pair, sent_other, pair_ref, other_ref, w_ref, one_ref, *refs
    ):
        mats, (est_ref, part_ref, to_pair, to_other, held) = refs[:7], refs[7:]
        even = is_even()
        has_lo, has_hi = has_sides()
        lo, hi = pick(even, pair0_ref, other0_ref, h)
        got_lo, got_hi = pick(even, pair_ref, other_ref)
        sent_lo, sent_hi = pick(even, sent_pair, sent_other)
        lo = lo * (one_ref[0:edge] + scale * (sent_lo[0:edge] + got_lo[0:edge]))
        hi = hi * (one_ref[edge + rows :] + scale * (sent_hi[edge:] + got_hi[edge:]))
        got = jnp.concatenate([got_lo[edge:], got_hi[0:edge]], axis=0)
        level = level_ref[0:1, 0:1]
        estimate = start_ref[...] * (one_ref[pl.ds(edge, rows)] + scale * (own_ref[...] + got))
        est_ref[...] = estimate
        shape = across(w_ref[...], lateral) * level
        shapes = jnp.concatenate([shape] * (edge // shape.shape[0]), axis=0)
        ext = jnp.concatenate(
            [
                lo - shapes * has_lo,
                estimate - jnp.concatenate([shape] * slab, axis=0),
                hi - shapes * has_hi,
            ],
            axis=0,
        )
        part = blur_back(views, slab, rows, level, data_ref.at[h], ext.astype(BF), mats, held)
        part_ref[...] = part[edge : edge + rows]
        put(even, part[0:edge], part[edge + rows :], to_pair, to_other)

    return kernel


def table_kernel(depth, lateral):
    half = lateral // 2

    def kernel(quarter_ref, wave_ref, _, waves_ref, back_ref, high_ref, low_ref):
        steps = [jnp.broadcast_to(quarter_ref[0:1, :], (8, 128)), jnp.broadcast_to(quarter_ref[1:2, :], (8, 128))]
        row8 = iota((8, 128), 0)
        odd_row = (iota((16, 128), 0) & 1) == 1
        odd_lane = (iota((16, 128), 1) & 1) == 1
        for j in range(half // 128):
            lane = iota((8, 128), 1) + j * 128
            phase = (row8 * lane) & (lateral - 1)
            for i in range(half // 16):
                pair = []
                for _ in range(2):
                    near, turn = phase & 127, phase // 128
                    g0 = jnp.take_along_axis(steps[0], near, axis=1)
                    g1 = jnp.take_along_axis(steps[1], near, axis=1)
                    odd = (turn & 1) == 1
                    cos = jnp.where(odd, g1, g0)
                    sin = jnp.where(odd, g0, g1)
                    pair.append((jnp.where(turn >= 2, -cos, cos), jnp.where((turn == 0) | (turn == 3), -sin, sin)))
                    phase = (phase + lane * 8) & (lateral - 1)
                cos = jnp.concatenate([pair[0][0], pair[1][0]], axis=0)
                sin = jnp.concatenate([pair[0][1], pair[1][1]], axis=0)
                ahead, behind = sin, -sin
                if j == 0:
                    ahead = jnp.where(iota((16, 128), 1) == 0, jnp.where(odd_row, -1.0, 1.0), sin)
                if i == 0:
                    behind = jnp.where(iota((16, 128), 0) == 0, jnp.where(odd_lane, -1.0, 1.0), behind)
                here, there = pl.ds(i * 16, 16), pl.ds(half + i * 16, 16)
                left, right = pl.ds(j * 128, 128), pl.ds(half + j * 128, 128)
                waves_ref[here, left] = cos.astype(BF)
                waves_ref[here, right] = ahead.astype(BF)
                waves_ref[there, left] = jnp.where(odd_lane, -cos, cos).astype(BF)
                waves_ref[there, right] = jnp.where(odd_lane, -ahead, ahead).astype(BF)
                back_ref[here, left] = cos.astype(BF)
                back_ref[here, right] = jnp.where(odd_row, -cos, cos).astype(BF)
                back_ref[there, left] = behind.astype(BF)
                back_ref[there, right] = jnp.where(odd_row, -behind, behind).astype(BF)
        slot = iota((depth, 128), 1) // depth
        group = 128 // depth
        for kind in range(2):
            wave = wave_ref[kind]
            high = wave.astype(BF).astype(F32)
            for i in range(group):
                at = pl.ds((kind * group + i) * depth, depth)
                here = slot == i
                high_ref[at, :] = jnp.where(here, high, 0.0).astype(BF)
                low_ref[at, :] = jnp.where(here, wave - high, 0.0).astype(BF)

    return kernel


def z_waves(table_hi, table_lo, x):
    cosines, sines = [], []
    for at in range(0, x.shape[0], 128):
        part = x[at : at + 128]
        high = part.astype(BF)
        low = (part - high.astype(F32)).astype(BF)
        total = dot(table_hi, high) + dot(table_hi, low) + dot(table_lo, high)
        cosines.append(total[:128])
        sines.append(total[128:])
    return jnp.concatenate(cosines, axis=0), jnp.concatenate(sines, axis=0)


def spectrum(even, scale, rows, half, est_ref, part_ref, pair_ref, other_ref, one_ref, waves_ref, high_ref, low_ref):
    got_lo, got_hi = pick(even, pair_ref, other_ref)
    got = jnp.concatenate([got_lo, got_hi], axis=0)
    estimate = est_ref[...] * (one_ref[...] + scale * (part_ref[...] + got))
    row = dot(estimate.astype(BF), waves_ref[...])
    cos_cos, cos_sin = z_waves(high_ref[...], low_ref[...], row[:, :half])
    sin_cos, sin_sin = z_waves(high_ref[...], low_ref[...], row[:, half:])
    first = iota((rows, half), 1) == 0
    real = cos_cos - jnp.where(first, 0.0, sin_sin)
    imag = -cos_sin - jnp.where(first, 0.0, sin_cos)
    top = iota((rows, 128), 1) == 0
    top_real = jnp.where(top, sin_cos[:, :128], 0.0)
    top_imag = jnp.where(top, -sin_sin[:, :128], 0.0)
    return real, imag, top_real, top_imag


def spectrum_kernel(views, slab, depth, lateral):
    rows, half = slab * depth, lateral // 2

    def kernel(est_ref, part_ref, pair_ref, other_ref, one_ref, waves_ref, high_ref, low_ref, *outs):
        even = is_even()
        args = (est_ref, part_ref, pair_ref, other_ref, one_ref, waves_ref, high_ref, low_ref)
        values = spectrum(even, 1.0 / views, rows, half, *args)
        for ref, value in zip(outs, values):
            ref[...] = value
        power = values[0] * values[0] + values[1] * values[1]
        total = power[0:depth]
        for s in range(1, slab):
            total = total + power[s * depth : (s + 1) * depth]
        outs[4][...] = total * jnp.where(iota((depth, half), 1) == 0, 1.0, 2.0)

    return kernel


def cycle_kernel(depth, half):
    def kernel(map_ref, _, cycle_ref):
        columns = jnp.transpose(map_ref[0, :, 0:half].astype(F32))
        cycle = iota((128, CYCLES), 1).astype(F32)
        zero = jnp.zeros((128, 128), BF)
        for k in range(depth // 2 + 1):
            low = columns[:128, k : k + 1] == cycle
            high = columns[128:, k : k + 1] == cycle[:, 128:]
            cycle_ref[pl.ds(k * half, 128), :] = jnp.where(low, 1.0, 0.0).astype(BF)
            cycle_ref[pl.ds(k * half + 128, 128), 0:128] = zero
            cycle_ref[pl.ds(k * half + 128, 128), 128:256] = jnp.where(high, 1.0, 0.0).astype(BF)

    return kernel


def power_kernel(views, slab, depth, lateral, count):
    rows, half = slab * depth, lateral // 2

    def kernel(
        est_ref,
        part_ref,
        pair_ref,
        other_ref,
        one_ref,
        waves_ref,
        high_ref,
        low_ref,
        cycle_ref,
        re_ref,
        im_ref,
        tre_ref,
        tim_ref,
        power_ref,
        mre_ref,
        mim_ref,
        mtre_ref,
        mtim_ref,
        sum_ref,
    ):
        even = is_even()
        args = (est_ref, part_ref, pair_ref, other_ref, one_ref, waves_ref, high_ref, low_ref)
        re1, im1, tre1, tim1 = spectrum(even, 1.0 / views, rows, half, *args)
        re0, im0, tre0, tim0 = re_ref[...], im_ref[...], tre_ref[...], tim_ref[...]
        mre_ref[...] = 0.5 * (re0 + re1)
        mim_ref[...] = 0.5 * (im0 + im1)
        mtre_ref[...] = 0.5 * (tre0 + tre1)
        mtim_ref[...] = 0.5 * (tim0 + tim1)

        def over_slab(x):
            total = x[0:depth]
            for s in range(1, slab):
                total = total + x[s * depth : (s + 1) * depth]
            return total

        twice = jnp.where(iota((depth, half), 1) == 0, 1.0, 2.0)
        powers, tops = [], []
        for a, b, c, d in (
            (re0, re1, im0, im1),
            (re1, re1, im1, im1),
        ):
            powers.append(over_slab(a * b + c * d) * twice)
        powers.insert(1, power_ref[...])
        for a, b, c, d in (
            (tre0, tre1, tim0, tim1),
            (tre0, tre0, tim0, tim0),
            (tre1, tre1, tim1, tim1),
        ):
            tops.append(jnp.sum(over_slab(a * b + c * d), axis=0, keepdims=True))
        top = jnp.sum(jnp.concatenate(tops, axis=0), axis=1, keepdims=True)
        terms = []
        for k in range(depth // 2 + 1):
            other = depth - k
            fold = [p[k : k + 1] + p[other : other + 1] if 0 < k < other else p[k : k + 1] for p in powers]
            terms.append(jnp.concatenate(fold, axis=0))
        term = jnp.concatenate(terms, axis=1)
        high = term.astype(BF).astype(F32)
        middle = (term - high).astype(BF).astype(F32)
        low = term - high - middle
        total = dot(jnp.concatenate([high, middle, low], axis=0).astype(BF), cycle_ref[...])
        last = jnp.where(iota((3, CYCLES), 1) == CYCLES - 1, top, 0.0)
        total = total[0:3] + total[3:6] + total[6:9] + last
        for i in range(count):
            sum_ref[i] = total

    return kernel


def inverse_kernel(slab, depth, lateral, count):
    half = lateral // 2

    def kernel(cut_ref, sum_ref, map_ref, mre_ref, mim_ref, mtre_ref, mtim_ref, back_ref, high_ref, low_ref, out_ref, held, sems):
        total = sum_ref[0]
        for i in range(1, count):
            total = total + sum_ref[i]
        cross, power0, power1 = total[0:1], total[1:2], total[2:3]
        corr = cross / (jnp.sqrt(power0) * jnp.sqrt(power1))
        weight = jnp.where(iota((1, CYCLES), 1) <= cut_ref[0], corr, 0.0)
        low = jnp.broadcast_to(weight[:, 0:128], (depth, 128))
        high = jnp.broadcast_to(weight[:, 128:256], (depth, 128))
        pieces = []
        for j in range(half // 128):
            cell = map_ref[0, :, pl.ds(j * 128, 128)]
            near = cell & 127
            found = jnp.where(
                cell < 128,
                jnp.take_along_axis(low, near, axis=1),
                jnp.take_along_axis(high, near, axis=1),
            )
            twice = jnp.where(iota((depth, 128), 1) + j * 128 == 0, 1.0, 2.0)
            pieces.append(found * twice)
        cells = jnp.concatenate(pieces, axis=1)
        cells = jnp.concatenate([cells] * slab, axis=0)
        last = weight[:, CYCLES - 1 : CYCLES]
        re = mre_ref[...] * cells
        im = mim_ref[...] * cells
        re = jnp.concatenate([re[:, :128] - mtim_ref[...] * last, re[:, 128:]], axis=1)
        im = jnp.concatenate([im[:, :128] + mtre_ref[...] * last, im[:, 128:]], axis=1)
        re_cos, re_sin = z_waves(high_ref[...], low_ref[...], re)
        im_cos, im_sin = z_waves(high_ref[...], low_ref[...], im)
        inner_re = (re_cos - im_sin).astype(BF)
        inner_im = (re_sin + im_cos).astype(BF)
        copies = []
        for j in range(2):
            at = pl.ds(j * half, half)
            joined = dot(inner_re, back_ref[0:half, at]) + dot(inner_im, back_ref[half:lateral, at])
            held[j] = joined * (1.0 / (depth * lateral))
            copies.append(pltpu.make_async_copy(held.at[j], out_ref.at[:, at], sems.at[j]))
            copies[j].start()
        for copy in copies:
            copy.wait()

    return kernel


def body(data_halves, psf_taps, cycle_map, cutoff):
    _, views, slab, depth, lateral = data_halves.shape
    taps = psf_taps.shape[-1]
    radius = taps // 2
    rows, edge = slab * depth, radius * depth
    ext_rows = rows + 2 * edge
    half = lateral // 2
    count = lax.axis_size("tile")
    pairs = [(i, i ^ 1) for i in range(count)]
    others = [(i, i + 1) for i in range(1, count - 1, 2)]
    others = others + [(b, a) for a, b in others]

    def to_other(array):
        return lax.ppermute(array, "tile", others)

    def to_pair(array):
        return lax.ppermute(array, "tile", pairs)

    def exchange(for_pair, for_other):
        other = to_other(for_other)
        return to_pair(for_pair), other

    vmem = pl.BlockSpec(memory_space=pltpu.VMEM)
    scalars = pl.BlockSpec(memory_space=pltpu.SMEM)

    def call(kernel, inputs, outputs, scratch=(), flops=0):
        bytes_moved = sum(int(np.prod(s.shape)) * s.dtype.itemsize for s in outputs)
        return pl.pallas_call(
            kernel,
            in_specs=[x[1] if isinstance(x, tuple) else vmem for x in inputs],
            out_specs=tuple(vmem for _ in outputs),
            out_shape=tuple(outputs),
            scratch_shapes=list(scratch),
            cost_estimate=pl.CostEstimate(flops=flops, bytes_accessed=2 * bytes_moved, transcendentals=0),
            compiler_params=pltpu.CompilerParams(vmem_limit_bytes=VMEM_LIMIT),
        )(*[x[0] if isinstance(x, tuple) else x for x in inputs])

    def shaped(*shape, dtype=F32):
        return jax.ShapeDtypeStruct(shape, dtype)

    data = data_halves.reshape(2, views, rows, lateral)
    side = shaped(1, edge, lateral, dtype=BF)
    plane = shaped(rows, lateral)
    begun = call(
        edge_kernel(views, rows, edge),
        [data],
        [plane, shaped(rows, lateral, dtype=BF), shaped(8, 128), side] * 2
        + [shaped(2, edge, lateral, dtype=BF)],
        flops=10**9,
    )
    means, own_exts, levels = begun[0:8:4], begun[1:8:4], begun[2:8:4]
    others0 = [to_other(begun[3]), to_other(begun[7])]
    pair0 = to_pair(begun[8])
    starts = [(pair0, other) for other in others0]

    band = shaped(views, 256, 256, dtype=BF)
    base, offset = shaped(views * rows, 128), shaped(views, depth, 128)
    psf = pltpu.with_memory_space_constraint(psf_taps.transpose(1, 0, 2), pltpu.HBM)
    psf = (psf, pl.BlockSpec(memory_space=pltpu.HBM))
    taps_here = [pltpu.VMEM((3, views, taps), F32), pltpu.SemaphoreType.DMA]
    *mats, kept = call(
        prep_kernel(False, views, taps, slab, depth, lateral),
        [psf],
        [
            shaped(views * rows // 2, rows // 2 + 2 * edge, dtype=BF),
            shaped(rows // 2 + 2 * edge, views * rows // 2, dtype=BF),
            band,
            band,
            base,
            offset,
            shaped(views, 2, 8, lateral),
            shaped(3, views, taps),
        ],
        taps_here,
        flops=4 * 10**9,
    )
    base1, offset1, shape, one0, one1 = call(
        prep_kernel(True, views, taps, slab, depth, lateral),
        [kept, mats[6]],
        [base, offset, shaped(depth, 128), shaped(ext_rows, lateral), shaped(rows, lateral)],
        flops=10**9,
    )
    mats1 = [*mats[:4], base1, offset1, mats[6]]

    held = [pltpu.VMEM((2, views * rows // 2, lateral), BF)]
    firsts = []
    for h in range(2):
        own, for_pair, for_other = call(
            first_kernel(h, views, slab, rows, edge),
            [data, own_exts[h], levels[h], *starts[h], *mats],
            [shaped(rows, lateral)] + [shaped(1, 2 * edge, lateral, dtype=BF)] * 2,
            held,
            flops=4 * 10**9,
        )
        firsts.append((own, for_pair, for_other) + exchange(for_pair, for_other))

    angle = 2.0 * np.pi / lateral * np.arange(256)
    quarter = jnp.asarray(np.cos(angle).astype(np.float32).reshape(2, 128))
    grid_z = np.arange(depth)[:, None] * np.arange(depth)[None, :] % depth * (2.0 * np.pi / depth)
    wave = np.stack([np.cos(grid_z), np.sin(grid_z)]).astype(np.float32)
    wave = jnp.asarray(np.tile(wave, (1, 1, 128 // depth)))
    table = shaped(256, 128, dtype=BF)
    seconds = []
    for h in range(2):
        est, part, for_pair, for_other = call(
            second_kernel(h, views, slab, rows, edge, lateral),
            [data, means[h], levels[h], *starts[h]]
            + [*firsts[h], shape, one0]
            + mats1,
            [shaped(rows, lateral)] * 2 + [shaped(1, edge, lateral, dtype=BF)] * 2,
            held,
            flops=4 * 10**9,
        )
        seconds.append((est, part) + exchange(for_pair, for_other))

    waves, back, table_hi, table_lo = call(
        table_kernel(depth, lateral),
        [quarter, wave, seconds[1][0]],
        [shaped(lateral, lateral, dtype=BF), shaped(lateral, lateral, dtype=BF), table, table],
        flops=2 * 10**9,
    )

    (cycles,) = call(
        cycle_kernel(depth, half),
        [cycle_map, seconds[1][0]],
        [shaped((depth // 2 + 1) * half, CYCLES, dtype=BF)],
        flops=10**9,
    )

    plane, top = shaped(rows, half), shaped(rows, 128)
    tables = [one1, waves, table_hi, table_lo]
    spectra = call(
        spectrum_kernel(views, slab, depth, lateral),
        [*seconds[0]] + tables,
        [plane, plane, top, top, shaped(depth, half)],
        flops=10**9,
    )
    *mixed, sums = call(
        power_kernel(views, slab, depth, lateral, count),
        [*seconds[1]] + tables + [cycles, *spectra],
        [plane, plane, top, top, shaped(count, 3, CYCLES)],
        flops=2 * 10**9,
    )
    sums = lax.all_to_all(sums, "tile", 0, 0)
    joined = pl.pallas_call(
        inverse_kernel(slab, depth, lateral, count),
        in_specs=[scalars] + [vmem] * 9,
        out_specs=pl.BlockSpec(memory_space=pl.ANY),
        out_shape=shaped(rows, lateral),
        scratch_shapes=[pltpu.VMEM((2, rows, half), F32), pltpu.SemaphoreType.DMA((2,))],
        cost_estimate=pl.CostEstimate(flops=10**9, bytes_accessed=10**6, transcendentals=0),
        compiler_params=pltpu.CompilerParams(vmem_limit_bytes=VMEM_LIMIT),
        name="inverse",
    )(cutoff, sums, cycle_map, *mixed, back, table_hi, table_lo)
    return joined.reshape(slab, depth, lateral)


def solution(mesh):
    in_specs = (
        P(None, None, ("groups", "tile"), None, None),
        P(),
        P(("groups", "tile"), None, None),
        P("groups"),
    )
    out_specs = P(("groups", "tile"), None, None)

    return jax.shard_map(body, mesh=mesh, in_specs=in_specs, out_specs=out_specs, check_vma=False)
```
